32 devices in a mesh: row: 8 (over y, x, core), col: 4 (over z).
Axes of the slice: x: 2, y: 2, z: 4, core: 2. Of those that a mesh axis runs over, the one named last changes fastest.
Arguments:
- tokens: bfloat16 [128, 96, 768], P('row', 'col'), as said below
- dw_kernel: float32 [7, 7, 768], replicated, may hold values from -0.875 to 0.875
- norm_gain: float32 [768], replicated, may hold values from 0.5 to 1.5
- norm_shift: float32 [768], replicated, may hold values from -3 to 3
- w_in: bfloat16 [768, 3072], P(None, 'col'), may hold values from -0.21875 to 0.21875
- w_out: bfloat16 [3072, 768], P('col'), may hold values from -0.109375 to 0.109375
- w_kv: bfloat16 [768, 1536], P(None, 'col'), as said below
- queries: bfloat16 [512, 768], replicated, may hold values from -300 to 300, as said below
- latent_gain: float32 [768], replicated, may hold values from 0.5 to 1.5
- w_o: bfloat16 [768, 768], P(None, 'col'), may hold values from -0.21875 to 0.21875
Outputs:
- token_map: bfloat16 [128, 96, 768], P('row', 'col')
- latents: bfloat16 [512, 768], replicated
The draws below stay inside these ranges and needn't reach their ends.
Inputs may be any that keep to these rules, and one draw needn't show every extreme that they name: Latent queries; a few rows may be far larger than the others. `tokens`: patch token features, roughly unit normal, between -24 and 24; a few cells hold 24 in two channels. `w_kv`: key and value projection weights.
All inputs are finite; a program needn't handle non-finite values.
Results may differ from the reference program's by a relative error of at most 0.011.
Values may be sent and summed in bfloat16 or wider, within the bound.
A program may use at most 64 MiB of HBM per device.

```python
import math
import jax
import jax.numpy as jnp
from jax import lax

D = 768
FF = 3072
HEADS = 12
HEAD = 64
LATENTS = 512
HD = 16
WD = 24
H = 128
W = 96


def kv_matrix(key):
    values = jax.random.normal(jax.random.fold_in(key, 21), (D, 2 * D), jnp.float32)
    return jnp.clip(values, -6.0, 6.0) / jnp.sqrt(jnp.float32(D))


def channel_pairs():
    latent_ids = jnp.arange(LATENTS, dtype=jnp.int32)
    first = latent_ids % D
    second = (first + 1 + latent_ids // D) % D
    return (latent_ids, first, second)


def draw_w_kv(key, part):
    return kv_matrix(key).astype(jnp.bfloat16)


def draw_tokens(key, part):
    base = jax.random.normal(jax.random.fold_in(key, 31), (H, W, D), jnp.float32)
    base = jnp.clip(base, -6.0, 6.0)
    latent_ids, first, second = channel_pairs()
    grid_cols = W // WD
    device_count = H // HD * grid_cols
    per_device = LATENTS // device_count
    owner = latent_ids // per_device
    target = (owner + device_count // 2) % device_count
    slot = latent_ids % per_device
    row_pos = target // grid_cols * HD + slot // WD
    col_pos = target % grid_cols * WD + slot % WD
    base = base.at[row_pos, col_pos, first].set(24.0)
    base = base.at[row_pos, col_pos, second].set(24.0)
    return base.astype(jnp.bfloat16)


def draw_queries(key, part):
    matrix = kv_matrix(key)
    latent_ids, first, second = channel_pairs()
    aligned = 48.0 * (matrix[first, :D] + matrix[second, :D])
    noise = jnp.clip(jax.random.normal(jax.random.fold_in(key, 11), (LATENTS, D), jnp.float32), -5.0, 5.0)
    values = aligned + 0.5 * noise
    return values.astype(jnp.bfloat16)


def block_levels(own_key, shape, cuts, least, top_value):
    def one(dim, blocks):
        heights = jax.random.uniform(jax.random.fold_in(jax.random.fold_in(own_key, 6), dim), (blocks,), jnp.float32, least / len(cuts), top_value / len(cuts))
        return jnp.repeat(jnp.exp(heights), shape[dim] // blocks).reshape((-1,) + (1,) * (len(shape) - dim - 1))

    factor_of = one(*cuts[0])
    for cut in cuts[1:]:
        factor_of = factor_of * one(*cut)
    return factor_of


def gaussian(key, extent, deviation, limit, split=(), kind=jnp.bfloat16):
    array = jax.random.normal(key, extent, jnp.float32) * deviation
    if len(split) > 0:
        array = block_levels(key, extent, split, -0.22, 0.18) * array
    return jnp.clip(array, min=-limit, max=limit).astype(kind)


def setup_inputs(seed: int = 0) -> dict:
    splits = jax.random.split(jax.random.key(seed), 11)
    tokens = draw_tokens(jax.random.fold_in(splits[10], 71), 0)
    dw_kernel = gaussian(splits[1], (7, 7, D), 49 ** -0.5, 0.875, (), jnp.float32)
    norm_gain = jnp.clip(1.0 + 0.1 * jax.random.normal(splits[2], (D,), jnp.float32), 0.5, 1.5)
    norm_shift = gaussian(splits[3], (D,), 0.5, 3.0, (), jnp.float32)
    w_in = gaussian(splits[4], (D, FF), D ** -0.5, 0.21875, ((1, 4),))
    w_out = gaussian(splits[5], (FF, D), FF ** -0.5, 0.109375, ((0, 4),))
    w_kv = draw_w_kv(jax.random.fold_in(splits[10], 71), 0)
    queries = draw_queries(jax.random.fold_in(splits[10], 71), 0)
    latent_gain = jnp.clip(1.0 + 0.1 * jax.random.normal(splits[8], (D,), jnp.float32), 0.5, 1.5)
    w_o = gaussian(splits[9], (D, D), D ** -0.5, 0.21875, ((1, 4),))
    return {"tokens": tokens, "dw_kernel": dw_kernel, "norm_gain": norm_gain, "norm_shift": norm_shift, "w_in": w_in, "w_out": w_out, "w_kv": w_kv, "queries": queries, "latent_gain": latent_gain, "w_o": w_o}


def conv_taps(padded, height, width, dw_kernel):
    mixed = jnp.zeros((height, width, padded.shape[2]), jnp.float32)
    for row_tap in range(7):
        for col_tap in range(7):
            mixed = mixed + padded[row_tap:row_tap + height, col_tap:col_tap + width] * dw_kernel[row_tap, col_tap]
    return mixed

def layer_norm(mixed, norm_gain, norm_shift):
    center = mixed - lax.optimization_barrier(jnp.mean(mixed, axis=-1, keepdims=True))
    spread = lax.optimization_barrier(jnp.mean(center * center, axis=-1, keepdims=True))
    return (center * lax.rsqrt(spread + 1e-06) * norm_gain + norm_shift).astype(jnp.bfloat16)

def finish_latents(numer, denom, latent_gain, w_o):
    attended = (numer / denom[..., None]).reshape(numer.shape[0], -1)
    squares = lax.optimization_barrier(jnp.mean(attended * attended, axis=-1, keepdims=True))
    scaled = (attended * lax.rsqrt(squares + 1e-06) * latent_gain).astype(jnp.bfloat16)
    return jnp.dot(scaled, w_o, preferred_element_type=jnp.float32).astype(jnp.bfloat16)

def reference(tokens, dw_kernel, norm_gain, norm_shift, w_in, w_out, w_kv, queries, latent_gain, w_o):
    padded = jnp.pad(tokens.astype(jnp.float32), ((3, 3), (3, 3), (0, 0)))
    mixed = conv_taps(padded, H, W, dw_kernel)
    normed = layer_norm(mixed, norm_gain, norm_shift)
    block_rows = math.gcd(H * W, 4096)
    count = H * W // block_rows
    normed_blocks = normed.reshape(count, block_rows, D)
    token_blocks = tokens.reshape(count, block_rows, D)

    def mlp_block(pair):
        normed_rows, token_rows = pair
        hidden = jax.nn.gelu(jnp.dot(normed_rows, w_in, preferred_element_type=jnp.float32)).astype(jnp.bfloat16)
        update = jnp.dot(hidden, w_out, preferred_element_type=jnp.float32)
        output = (token_rows.astype(jnp.float32) + update).astype(jnp.bfloat16)
        keys_vals = jnp.dot(output, w_kv, preferred_element_type=jnp.float32).astype(jnp.bfloat16)
        return (output, keys_vals)
    out_blocks, kv_blocks = lax.map(mlp_block, (normed_blocks, token_blocks))
    token_map = out_blocks.reshape(H, W, D)
    query_heads = queries.astype(jnp.float32).reshape(LATENTS, HEADS, HEAD)
    score_scale = 1.0 / math.sqrt(HEAD)

    def block_scores(kv_block):
        key_heads = kv_block[:, :D].astype(jnp.float32).reshape(-1, HEADS, HEAD)
        return jnp.einsum('lhd,thd->lht', query_heads, key_heads, precision=lax.Precision.HIGHEST) * score_scale

    def block_max(kv_block):
        return lax.optimization_barrier(jnp.max(block_scores(kv_block), axis=-1))
    maxima = lax.optimization_barrier(jnp.max(lax.map(block_max, kv_blocks), axis=0))

    def accumulate(running, kv_block):
        denom, numer = running
        weights = jnp.exp(block_scores(kv_block) - maxima[..., None])
        denom = denom + lax.optimization_barrier(jnp.sum(weights, axis=-1))
        rounded = lax.optimization_barrier(weights.astype(jnp.bfloat16)).astype(jnp.float32)
        val_heads = kv_block[:, D:].astype(jnp.float32).reshape(-1, HEADS, HEAD)
        numer = numer + jnp.einsum('lht,thd->lhd', rounded, val_heads, precision=lax.Precision.HIGHEST)
        return ((denom, numer), None)
    start = (jnp.zeros((LATENTS, HEADS), jnp.float32), jnp.zeros((LATENTS, HEADS, HEAD), jnp.float32))
    (denom, numer), unused = lax.scan(accumulate, start, kv_blocks)
    latents = finish_latents(numer, denom, latent_gain, w_o)
    return (token_map, latents)
```

```python
import functools
import math

import jax
import jax.numpy as jnp
from jax import lax
from jax.experimental import pallas as pl
from jax.experimental.pallas import tpu as pltpu
from jax.sharding import PartitionSpec as P

HEADS = 12
HEAD = 64
HALO = 3
EDGE = 8
LANES = 128
MESH = pl.DeviceIdType.MESH
VMEM_BYTES = 60 * 1024 * 1024


LAG_B = 2
LAG_C = 4


def block_kernel(
    rows,
    cols,
    tokens_in,
    dw_in,
    gain,
    shift,
    w_in,
    w_out,
    w_kv,
    w_o,
    queries_in,
    latent_gain,
    tok_out,
    lat,
    tokens,
    dw,
    queries,
    g_in,
    g_out,
    g_kv,
    g_o,
    pad,
    mixed,
    normed,
    hidden,
    acc,
    tok_map,
    tok_bf,
    kv,
    h_rows,
    h_cols,
    h_corners,
    num,
    stat,
    got,
    att,
    halo_send,
    halo_recv,
    z_send,
    z_recv,
    hop_send,
    hop_recv,
    tok_send,
    tok_recv,
    sum_send,
    sum_recv,
    out_send,
    out_recv,
    local_sem,
):
    row, col = lax.axis_index("row"), lax.axis_index("col")
    height, width, depth = tokens.shape
    count = height * width
    y, x, core = row // 4, (row // 2) % 2, row % 2
    chip = row // 2
    half = depth // 2
    x_row = row + 2 * (1 - 2 * x)
    y_row = row + 4 * (1 - 2 * y)
    d_row = row + 2 * (1 - 2 * x) + 4 * (1 - 2 * y)
    mate = row + 1 - 2 * core

    barrier = pltpu.get_barrier_semaphore()
    for i in range(rows):
        for j in range(cols):
            if i or j:
                pl.semaphore_signal(
                    barrier,
                    inc=1,
                    device_id=((row + i) % rows, (col + j) % cols),
                    device_id_type=MESH,
                )

    def remote(src, dst, send, recv, device):
        return pltpu.make_async_remote_copy(
            src_ref=src,
            dst_ref=dst,
            send_sem=send,
            recv_sem=recv,
            device_id=device,
            device_id_type=MESH,
        )

    def local(src, dst, i):
        return pltpu.make_async_copy(src, dst, local_sem.at[i])

    core_lanes = pl.ds(pl.multiple_of(core * half, LANES), half)
    tokens_copy = local(tokens_in, tokens, 0)
    dw_copy = local(dw_in, dw, 1)
    queries_copy = local(queries_in.at[:, core_lanes], queries, 2)
    in_copy = local(w_in, g_in.at[col], 3)
    out_copy = local(w_out, g_out.at[col], 4)
    kv_copy = local(w_kv, g_kv.at[col // 2], 5)
    o_copy = local(w_o, g_o.at[col % 2], 6)
    for copy in (tokens_copy, dw_copy, queries_copy, in_copy, out_copy):
        copy.start()

    @pl.when(col % 2 == core)
    def _():
        kv_copy.start()

    @pl.when(col // 2 == core)
    def _():
        o_copy.start()

    both = jnp.minimum(col, cols - 1 - col)
    longer = jnp.where(cols - 1 - col > col, 1, -1)
    blocks = []
    for k in range(cols - 1):
        paired = k < 2 * both
        side = jnp.where(paired, 1 - 2 * (k % 2), longer)
        gap = jnp.where(paired, k // 2 + 1, k - both + 1)
        blocks.append(col + side * gap)

    halo = []
    for dr in (-1, 0, 1):
        for dc in (-1, 0, 1):
            if dr == 0 and dc == 0:
                continue
            cond = None
            for d, pos, n in ((dr, row, rows), (dc, col, cols)):
                if d:
                    one = (pos + d >= 0) & (pos + d < n)
                    cond = one if cond is None else cond & one
            halo.append((dr, dc, cond))

    def halo_slot(dr, dc):
        if dc == 0:
            return h_rows.at[0 if dr < 0 else 1]
        if dr == 0:
            return h_cols.at[0 if dc < 0 else 1]
        return h_corners.at[(0 if dr < 0 else 2) + (0 if dc < 0 else 1)]

    def halo_copy(i, dr, dc):
        r_span = {-1: pl.ds(0, HALO), 0: slice(None), 1: pl.ds(height - HALO, HALO)}[dr]
        c_span = {-1: pl.ds(0, EDGE), 0: slice(None), 1: pl.ds(width - EDGE, EDGE)}[dc]
        return remote(
            tokens.at[r_span, c_span],
            halo_slot(-dr, -dc),
            halo_send.at[i],
            halo_recv.at[len(halo) - 1 - i],
            (row + dr, col + dc),
        )

    def own_unit(part):
        if part < 4:
            w = (w_in, w_out)[part // 2]
            return w.at[y, x, core, part % 2], (g_in, g_out)[part // 2].at[col, y, x, core, part % 2]
        if part < 6:
            return w_kv.at[y, x, part - 4], g_kv.at[col // 2, y, x, part - 4]
        return w_o.at[y, x], g_o.at[col % 2, y, x]

    def z_id(block, part):
        if part < 4:
            return block * 4 + part
        if part < 6:
            return 4 * cols + (block // 2) * 2 + part - 4
        return 4 * cols + 4 + block % 2

    def z_copy(k, part):
        src, dst = own_unit(part)
        return remote(
            src, dst, z_send.at[k * 7 + part], z_recv.at[z_id(col, part)], (row, blocks[k])
        )

    z_order = [(k, p) for k in range(cols - 1) for p in range(4)]
    z_order += [(k, p) for k in range(cols - 1) for p in (4, 5)]
    z_order += [(k, 6) for k in range(cols - 1)]

    def z_each(group, act):
        for k, p in group:
            cond = None if p < 4 else (col % 2 == core if p < 6 else col // 2 == core)
            if cond is None:
                act(z_copy(k, p))
            else:

                @pl.when(cond)
                def _():
                    act(z_copy(k, p))

    near = jnp.where(col < cols // 2, core, core + 2)
    far = jnp.where(col < cols // 2, core + 2, core)
    jobs = [(blocks[k], p) for k in range(cols - 1) for p in range(4)]
    ff_jobs = len(jobs)
    jobs += [(near, 4), (near, 5), (far, 4), (far, 5)]
    jobs += [(core * 2, 6), (core * 2 + 1, 6)]

    def unit(j, dy, dx):
        block, part = jobs[j]
        yy, xx = (1 - y if dy else y), (1 - x if dx else x)
        if part < 4:
            return (g_in, g_out)[part // 2].at[block, yy, xx, core, part % 2]
        if part < 6:
            return g_kv.at[block // 2, yy, xx, part - 4]
        return g_o.at[block % 2, yy, xx]

    def turn(j):
        part = jobs[j][1]
        return j % 2 if part == 6 else part % 2

    def hop(j, leg):
        at = j * 4 + leg
        if leg == 3:
            block, part = jobs[j]
            ref = (g_in, g_out)[part // 2].at[block, :, :, core, part % 2]
            device = mate
        elif leg == 2:
            ref = unit(j, 0, 1) if turn(j) == 0 else unit(j, 1, 0)
            device = y_row if turn(j) == 0 else x_row
        else:
            ref = unit(j, 0, 0)
            device = x_row if leg == 0 else y_row
        return remote(ref, ref, hop_send.at[at], hop_recv.at[at], (device, col))

    def landed(j, leg):
        at = j * 4 + leg
        if leg == 3:
            block, part = jobs[j]
            ref = (g_in, g_out)[part // 2].at[block, :, :, 1 - core, part % 2]
        elif leg == 2:
            ref = unit(j, 1, 1)
        else:
            ref = unit(j, 0, 1) if leg == 0 else unit(j, 1, 0)
        return remote(ref, ref, hop_send.at[at], hop_recv.at[at], (mate, col))

    def given(j, act):
        if j < ff_jobs:
            act()
        else:
            pl.when(jobs[j][0] != col)(act)

    def step_a(j):
        block, part = jobs[j]
        ref = unit(j, 0, 0)
        remote(ref, ref, z_send.at[0], z_recv.at[z_id(block, part)], (mate, col)).wait_recv()
        hop(j, 0).start()
        hop(j, 1).start()

    def step_b(j):
        landed(j, turn(j)).wait_recv()
        hop(j, 2).start()

    def step_c(j):
        landed(j, 1 - turn(j)).wait_recv()
        landed(j, 2).wait_recv()
        if j < ff_jobs:
            hop(j, 3).start()

    state = {"tick": 0}

    def tick():
        t = state["tick"]
        if t >= len(jobs) + LAG_C:
            return
        state["tick"] = t + 1
        for step, lag in ((step_a, 0), (step_b, LAG_B), (step_c, LAG_C)):
            j = t - lag
            if 0 <= j < len(jobs):
                given(j, functools.partial(step, j))

    def finish(j):
        while state["tick"] <= j + LAG_C:
            tick()
        if j < ff_jobs:
            landed(j, 3).wait_recv()

    tokens_copy.wait()
    pad[pl.ds(HALO, height), pl.ds(EDGE, width), :] = tokens[...].astype(jnp.float32)
    pl.semaphore_wait(barrier, rows * cols - 1)

    first = 4
    z_each(z_order[:first], lambda c: c.start())
    for i, (dr, dc, cond) in enumerate(halo):

        @pl.when(cond)
        def _():
            halo_copy(i, dr, dc).start()

    z_each(z_order[first:], lambda c: c.start())
    tick()

    spans = {-1: (0, HALO), 0: (HALO, height), 1: (HALO + height, HALO)}
    lanes_of = {-1: (0, EDGE), 0: (EDGE, width), 1: (EDGE + width, EDGE)}
    for i, (dr, dc, cond) in enumerate(halo):
        r0, rn = spans[dr]
        c0, cn = lanes_of[dc]

        @pl.when(cond)
        def _():
            halo_copy(len(halo) - 1 - i, -dr, -dc).wait_recv()
            pad[pl.ds(r0, rn), pl.ds(c0, cn), :] = halo_slot(dr, dc)[...].astype(jnp.float32)

        @pl.when(jnp.logical_not(cond))
        def _():
            pad[pl.ds(r0, rn), pl.ds(c0, cn), :] = jnp.zeros((rn, cn, depth), jnp.float32)

    taps = 2 * HALO + 1
    chunks = depth // LANES
    dw_copy.wait()

    def conv_rows(first, n_rows):
        def one(step, carry):
            i = first + step // chunks
            q = pl.multiple_of((step % chunks) * LANES, LANES)
            sums = [None] * taps
            for a in range(taps):
                line = pad[i + a, :, pl.ds(q, LANES)]
                for b in range(taps):
                    lo = 0 if b < HALO else EDGE
                    hi = EDGE + width + (EDGE if b > HALO else 0)
                    term = line[lo:hi] * dw[a, pl.ds(b, 1), pl.ds(q, LANES)]
                    sums[b] = term if sums[b] is None else sums[b] + term
            total = sums[HALO]
            for b in range(taps):
                if b == HALO:
                    continue
                size = width + EDGE
                offset = EDGE - HALO + b - (0 if b < HALO else EDGE)
                total = total + pltpu.roll(sums[b], (size - offset) % size, 0)[:width]
            mixed[i, :, pl.ds(q, LANES)] = total
            return carry

        lax.fori_loop(0, n_rows * chunks, one, 0)

    group = 2
    span = group * width

    def norm_rows(g, carry):
        value = mixed[pl.ds(g * group, group), :, :].reshape(span, depth)
        center = value - jnp.mean(value, axis=-1, keepdims=True)
        spread = jnp.mean(center * center, axis=-1, keepdims=True)
        out = center * lax.rsqrt(spread + 1e-06) * gain[...][None, :] + shift[...][None, :]
        normed[pl.ds(pl.multiple_of(g * span, 16), span), :] = out.astype(jnp.bfloat16)
        return carry

    quarter = height // 4
    for part in range(4):
        conv_rows(part * quarter, quarter)
        tick()
    lax.fori_loop(0, height // group, norm_rows, 0)
    tick()
    in_copy.wait()
    out_copy.wait()

    def wide(ref, block, lo, size):
        value = ref[(block,) + (slice(None),) * (len(ref.shape) - 2) + (pl.ds(lo, size),)]
        return value.reshape(-1, size)

    f_width = w_in.shape[-1]
    tile = 256 if f_width % 256 == 0 else LANES

    def expand(block):
        def one(n, carry):
            lo = pl.multiple_of(n * tile, tile)
            u = jnp.dot(normed[...], wide(g_in, block, lo, tile), preferred_element_type=jnp.float32)
            hidden[:, pl.ds(lo, tile)] = jax.nn.gelu(u).astype(jnp.bfloat16)
            return carry

        lax.fori_loop(0, f_width // tile, one, 0)

    def contract(block, fresh):
        def one(n, carry):
            lo = pl.multiple_of(n * 256, 256)
            part = jnp.dot(
                hidden[...], wide(g_out, block, lo, 256), preferred_element_type=jnp.float32
            )
            if fresh:
                acc[:, pl.ds(lo, 256)] = part
            else:
                acc[:, pl.ds(lo, 256)] += part
            return carry

        lax.fori_loop(0, depth // 256, one, 0)

    expand(col)
    tick()
    contract(col, True)
    for k in range(cols - 1):
        finish(4 * k)
        finish(4 * k + 1)
        expand(blocks[k])
        finish(4 * k + 2)
        finish(4 * k + 3)
        contract(blocks[k], False)

    def close_rows(g, carry):
        base = pad[pl.ds(HALO + g * group, group), pl.ds(EDGE, width), :].reshape(span, depth)
        at = pl.ds(pl.multiple_of(g * span, 16), span)
        total = base + acc[at, :]
        tok_map[pl.ds(g * group, group), :, :] = total.reshape(group, width, depth).astype(jnp.bfloat16)
        tok_bf[0, at, :] = total.astype(jnp.bfloat16)
        return carry

    pieces = 2
    piece = count // pieces

    def tok_copy(n):
        at = pl.ds(n * piece, piece)
        return remote(tok_bf.at[0, at], tok_bf.at[1, at], tok_send.at[n], tok_recv.at[n], (mate, col))

    for n in range(pieces):
        lax.fori_loop(n * (height // group // pieces), (n + 1) * (height // group // pieces), close_rows, 0)
        tok_copy(n).start()
    tok_out_copy = local(tok_map, tok_out, 7)
    tok_out_copy.start()

    kv_width = w_kv.shape[-1]

    def project(block, side):
        def one(n, carry):
            lo = pl.multiple_of(n * LANES, LANES)
            out = jnp.dot(
                tok_bf[side], wide(g_kv, block // 2, lo, LANES), preferred_element_type=jnp.float32
            )
            kv[block // 2, pl.ds(side * count, count), pl.ds(lo, LANES)] = out.astype(jnp.bfloat16)
            return carry

        lax.fori_loop(0, kv_width // LANES, one, 0)

    @pl.when(col % 2 == core)
    def _():
        kv_copy.wait()

    finish(ff_jobs)
    finish(ff_jobs + 1)
    project(near, 0)
    for n in range(pieces):
        tok_copy(n).wait_recv()
    project(near, 1)
    finish(ff_jobs + 2)
    finish(ff_jobs + 3)
    for side in range(2):
        project(far, side)
    queries_copy.wait()

    latents = queries.shape[0]
    scale = 1.0 / math.sqrt(HEAD)
    lane = lax.broadcasted_iota(jnp.int32, (1, LANES), 1)
    pairs = half // LANES
    stat_lanes = pl.ds(half, LANES)
    step_rows = latents // 2
    share = latents // (rows // 2 * cols)

    def attend(pair):
        lanes = pl.ds(pair * LANES, LANES)

        def one(n, carry):
            at = pl.ds(pl.multiple_of(n * step_rows, 16), step_rows)
            q = queries[at, lanes]
            keys = kv[0, :, lanes]
            vals = kv[1, :, lanes]
            base = jnp.zeros((step_rows, LANES), jnp.float32) if pair == 0 else stat[at, :]
            outs = []
            for s in range(2):
                keep = (lane // HEAD) == s
                q_one = jnp.where(keep, q, jnp.zeros_like(q))
                scores = lax.dot_general(
                    q_one, keys, (((1,), (1,)), ((), ())), preferred_element_type=jnp.float32
                )
                top = jnp.max(scores, axis=-1, keepdims=True)
                weights = jnp.exp((scores - top) * scale)
                den = jnp.sum(weights, axis=-1, keepdims=True)
                outs.append(
                    jnp.dot(weights.astype(jnp.bfloat16), vals, preferred_element_type=jnp.float32)
                )
                base = jnp.where(lane == pair * 2 + s, top * scale, base)
                base = jnp.where(lane == pair * 2 + s + 8, den, base)
            num[at, lanes] = jnp.where(lane < HEAD, outs[0], outs[1]).astype(jnp.bfloat16)
            if pair < pairs - 1:
                stat[at, :] = base
            else:
                high = base.astype(jnp.bfloat16).astype(jnp.float32)
                rest = base - high
                mid = rest.astype(jnp.bfloat16).astype(jnp.float32)
                low = rest - mid
                out = high + pltpu.roll(mid, 16, 1) + pltpu.roll(low, 32, 1)
                num[at, stat_lanes] = out.astype(jnp.bfloat16)
            return carry

        lax.fori_loop(0, latents // step_rows, one, 0)

    peers = [(i, j) for i in range(rows // 2) for j in range(cols) if i or j]

    def sum_copy(i, j, part):
        to_chip, to_col = (chip + i) % (rows // 2), (col + j) % cols
        slot = i * cols + j
        give = pl.ds(pl.multiple_of((to_chip * cols + to_col) * share, 16), share)
        size = LANES if part < pairs - 1 else 2 * LANES
        lanes = pl.ds(part * LANES, size)
        at = slot * pairs + part
        return remote(
            num.at[give, lanes],
            got.at[slot, :, lanes],
            sum_send.at[at],
            sum_recv.at[at],
            (to_chip * 2 + core, to_col),
        )

    for pair in range(pairs):
        attend(pair)
        for i, j in peers:
            sum_copy(i, j, pair).start()
        if pair == 0:
            while state["tick"] < len(jobs) + LAG_C:
                tick()

    for i, (dr, dc, cond) in enumerate(halo):

        @pl.when(cond)
        def _():
            halo_copy(i, dr, dc).wait_send()

    z_each(z_order, lambda c: c.wait_send())

    def sent(j):
        for leg in range(4 if j < ff_jobs else 3):
            hop(j, leg).wait_send()

    for j in range(len(jobs)):
        given(j, functools.partial(sent, j))
    for n in range(pieces):
        tok_copy(n).wait_send()
    tok_out_copy.wait()

    @pl.when(col // 2 == core)
    def _():
        o_copy.wait()

    def own_rows(at_chip, at_col):
        return pl.ds(pl.multiple_of((at_chip * cols + at_col) * share, 16), share)

    def spread(factor):
        parts = []
        for pair in range(pairs):
            lo = jnp.broadcast_to(factor[:, 2 * pair : 2 * pair + 1], (share, LANES))
            hi = jnp.broadcast_to(factor[:, 2 * pair + 1 : 2 * pair + 2], (share, LANES))
            parts.append(jnp.where(lane < HEAD, lo, hi))
        return jnp.concatenate(parts, axis=-1)

    for i, j in peers:
        for part in range(pairs):
            sum_copy(i, j, part).wait_recv()
    mine = own_rows(chip, col)
    slots = [None] + [i * cols + j for i, j in peers]

    def source(slot, lanes):
        value = num[mine, lanes] if slot is None else got[slot, :, lanes]
        return value.astype(jnp.float32)

    stats = []
    for slot in slots:
        s = source(slot, stat_lanes)
        stats.append(s + (pltpu.roll(s, LANES - 16, 1) + pltpu.roll(s, LANES - 32, 1)))
    peak = functools.reduce(jnp.maximum, stats)
    den, total = None, None
    for slot, s in zip(slots, stats):
        factor = jnp.exp(s - peak)
        d = pltpu.roll(s, LANES - 8, 1) * factor
        t = source(slot, pl.ds(0, half)) * spread(factor)
        den = d if den is None else den + d
        total = t if total is None else total + t
    att[core] = total / spread(den)
    n_sum = len(slots) * pairs
    swap = remote(att.at[core], att.at[core], sum_send.at[n_sum], sum_recv.at[n_sum], (mate, col))
    swap.start()
    for i, j in peers:
        for part in range(pairs):
            sum_copy(i, j, part).wait_send()
    remote(
        att.at[1 - core], att.at[1 - core], sum_send.at[n_sum], sum_recv.at[n_sum], (mate, col)
    ).wait_recv()
    first, second = att[0], att[1]
    squares = (
        jnp.sum(first * first, axis=-1, keepdims=True)
        + jnp.sum(second * second, axis=-1, keepdims=True)
    ) / depth
    inverse = lax.rsqrt(squares + 1e-06)
    scaled = jnp.concatenate([first, second], axis=-1) * inverse * latent_gain[...][None, :]
    turned = g_o[...].reshape(half, depth)
    done = lax.dot_general(
        scaled.astype(jnp.bfloat16), turned, (((1,), (1,)), ((), ())), preferred_element_type=jnp.float32
    )
    lat[mine, core_lanes] = done.astype(jnp.bfloat16)

    planes = [col] + blocks
    chips = [chip, x_row // 2, y_row // 2, d_row // 2]
    ways = [x_row, y_row, d_row]

    def out_copy_z(k):
        ref = lat.at[mine, core_lanes]
        return remote(ref, ref, out_send.at[k], out_recv.at[col], (row, blocks[k]))

    base_p, base_c = cols, cols + 3 * cols

    def out_copy_plane(n, way):
        ref = lat.at[own_rows(chip, planes[n]), core_lanes]
        at = base_p + n * 3 + way
        return remote(ref, ref, out_send.at[at], out_recv.at[at], (ways[way], col))

    def out_landed_plane(n, way):
        ref = lat.at[own_rows(chips[way + 1], planes[n]), core_lanes]
        at = base_p + n * 3 + way
        return remote(ref, ref, out_send.at[at], out_recv.at[at], (mate, col))

    mate_lanes = pl.ds(pl.multiple_of((1 - core) * half, LANES), half)

    def out_copy_core(n, who, lanes):
        ref = lat.at[own_rows(chips[who], planes[n]), lanes]
        at = base_c + n * 4 + who
        return remote(ref, ref, out_send.at[at], out_recv.at[at], (mate, col))

    def fan(n):
        for way in range(3):
            out_copy_plane(n, way).start()
        out_copy_core(n, 0, core_lanes).start()

    for k in range(cols - 1):
        out_copy_z(k).start()
    fan(0)
    for k in range(cols - 1):
        ref = lat.at[own_rows(chip, blocks[k]), core_lanes]
        remote(ref, ref, out_send.at[0], out_recv.at[blocks[k]], (mate, col)).wait_recv()
        fan(k + 1)
    for n in range(cols):
        for way in range(3):
            out_landed_plane(n, way).wait_recv()
            out_copy_core(n, way + 1, core_lanes).start()
    swap.wait_send()
    for k in range(cols - 1):
        out_copy_z(k).wait_send()
    for n in range(cols):
        for way in range(3):
            out_copy_plane(n, way).wait_send()
    for n in range(cols):
        for who in range(4):
            out_copy_core(n, who, mate_lanes).wait_recv()
            out_copy_core(n, who, core_lanes).wait_send()


def hbm(n):
    return [pl.BlockSpec(memory_space=pl.ANY)] * n


def vmem(n):
    return [pl.BlockSpec(memory_space=pltpu.VMEM)] * n


def fits(mesh_rows, mesh_cols, tokens, w_in, w_out, w_kv, queries, w_o):
    height, width, depth = tokens.shape
    return (
        mesh_rows == 8
        and mesh_cols == 4
        and depth == HEADS * HEAD
        and depth % 256 == 0
        and depth % (2 * LANES) == 0
        and w_in.shape[1] % LANES == 0
        and w_out.shape[0] % (32 * mesh_rows) == 0
        and depth % (32 * mesh_rows) == 0
        and w_kv.shape[1] * 2 == depth
        and w_o.shape[1] % 64 == 0
        and w_o.shape[1] * mesh_cols == depth
        and queries.shape[0] % (16 * mesh_rows // 2 * mesh_cols) == 0
        and height % 4 == 0
        and width % 8 == 0
        and height * width % 32 == 0
    )


def kernel_body(tokens, dw_kernel, norm_gain, norm_shift, w_in, w_out, w_kv, queries, latent_gain, w_o):
    rows, cols = lax.axis_size("row"), lax.axis_size("col")
    height, width, depth = tokens.shape
    if not fits(rows, cols, tokens, w_in, w_out, w_kv, queries, w_o):
        return body(
            tokens, dw_kernel, norm_gain, norm_shift, w_in, w_out, w_kv, queries, latent_gain, w_o
        )
    count = height * width
    latents = queries.shape[0]
    f_width = w_in.shape[1]
    half = depth // 2
    bf16, f32 = jnp.bfloat16, jnp.float32

    def cut(w, lead):
        size = w.shape[0]
        for n in lead:
            size //= n
        return w.reshape(lead + (size, w.shape[1]))

    shards = [
        cut(w_in, (2, 2, 2, 2)),
        cut(w_out, (2, 2, 2, 2)),
        cut(w_kv, (2, 2, 2)),
        cut(w_o.T, (2, 2)),
    ]
    share = latents // (rows // 2 * cols)
    pairs = half // LANES
    n_jobs = 4 * (cols - 1) + 4 + 2
    n_sum = rows // 2 * cols * pairs + 1
    n_out = cols + 3 * cols + 4 * cols
    dma = pltpu.SemaphoreType.DMA
    return pl.pallas_call(
        functools.partial(block_kernel, rows, cols),
        out_shape=(
            jax.ShapeDtypeStruct(tokens.shape, bf16),
            jax.ShapeDtypeStruct((latents, depth), bf16),
        ),
        in_specs=hbm(2) + vmem(2) + hbm(5) + vmem(1),
        out_specs=(hbm(1)[0], vmem(1)[0]),
        scratch_shapes=[
            pltpu.VMEM(tokens.shape, bf16),
            pltpu.VMEM(dw_kernel.shape, f32),
            pltpu.VMEM((latents, half), bf16),
            pltpu.VMEM((cols,) + shards[0].shape, bf16),
            pltpu.VMEM((cols,) + shards[1].shape, bf16),
            pltpu.VMEM((2,) + shards[2].shape, bf16),
            pltpu.VMEM((2,) + shards[3].shape, bf16),
            pltpu.VMEM((height + 2 * HALO, width + 2 * EDGE, depth), f32),
            pltpu.VMEM((height, width, depth), f32),
            pltpu.VMEM((count, depth), bf16),
            pltpu.VMEM((count, f_width), bf16),
            pltpu.VMEM((count, depth), f32),
            pltpu.VMEM((height, width, depth), bf16),
            pltpu.VMEM((2, count, depth), bf16),
            pltpu.VMEM((2, 2 * count, half), bf16),
            pltpu.VMEM((2, HALO, width, depth), bf16),
            pltpu.VMEM((2, height, EDGE, depth), bf16),
            pltpu.VMEM((4, HALO, EDGE, depth), bf16),
            pltpu.VMEM((latents, half + LANES), bf16),
            pltpu.VMEM((latents, LANES), f32),
            pltpu.VMEM((rows // 2 * cols, share, half + LANES), bf16),
            pltpu.VMEM((2, share, half), f32),
            dma((8,)),
            dma((8,)),
            dma(((cols - 1) * 7,)),
            dma((4 * cols + 6,)),
            dma((n_jobs * 4,)),
            dma((n_jobs * 4,)),
            dma((2,)),
            dma((2,)),
            dma((n_sum,)),
            dma((n_sum,)),
            dma((n_out,)),
            dma((n_out,)),
            dma((8,)),
        ],
        compiler_params=pltpu.CompilerParams(
            collective_id=0, has_side_effects=True, vmem_limit_bytes=VMEM_BYTES
        ),
        name="block",
    )(
        tokens,
        dw_kernel,
        norm_gain,
        norm_shift,
        *shards,
        queries,
        latent_gain,
    )


def with_halo(cells, sides, width):
    for axis, dim in sides:
        count = lax.axis_size(axis)
        ends = count - 1
        head = lax.slice_in_dim(cells, 0, width, axis=dim)
        tail = lax.slice_in_dim(cells, cells.shape[dim] - width, cells.shape[dim], axis=dim)
        cells = jnp.concatenate(
            [
                lax.ppermute(tail, axis, [(i, (i + 1) % count) for i in range(ends)]),
                cells,
                lax.ppermute(head, axis, [((i + 1) % count, i) for i in range(ends)]),
            ],
            axis=dim,
        )
    return cells


def conv_taps(padded, height, width, dw_kernel):
    mixed = jnp.zeros((height, width, padded.shape[2]), jnp.float32)
    for row_tap in range(7):
        for col_tap in range(7):
            mixed = (
                mixed
                + padded[row_tap : row_tap + height, col_tap : col_tap + width]
                * dw_kernel[row_tap, col_tap]
            )
    return mixed


def layer_norm(mixed, norm_gain, norm_shift):
    center = mixed - jnp.mean(mixed, axis=-1, keepdims=True)
    spread = jnp.mean(center * center, axis=-1, keepdims=True)
    return (center * lax.rsqrt(spread + 1e-06) * norm_gain + norm_shift).astype(jnp.bfloat16)


def finish_latents(numer, denom, latent_gain, w_full):
    attended = (numer / denom[..., None]).reshape(numer.shape[0], -1)
    squares = jnp.mean(attended * attended, axis=-1, keepdims=True)
    scaled = (attended * lax.rsqrt(squares + 1e-06) * latent_gain).astype(jnp.bfloat16)
    return jnp.dot(scaled, w_full, preferred_element_type=jnp.float32).astype(jnp.bfloat16)


def body(tokens, dw_kernel, norm_gain, norm_shift, w_in, w_out, w_kv, queries, latent_gain, w_o):
    height, width, width_d = tokens.shape
    latent_count = queries.shape[0]
    padded = with_halo(tokens, (("row", 0), ("col", 1)), 3)
    mixed = conv_taps(padded.astype(jnp.float32), height, width, dw_kernel)
    normed = layer_norm(mixed, norm_gain, norm_shift).reshape(height * width, width_d)
    residual = tokens.reshape(height * width, width_d).astype(jnp.float32)
    hidden = jax.nn.gelu(
        jnp.dot(
            normed,
            lax.all_gather(w_in, "col", axis=1, tiled=True),
            preferred_element_type=jnp.float32,
        )
    ).astype(jnp.bfloat16)
    update = jnp.dot(
        hidden, lax.all_gather(w_out, "col", axis=0, tiled=True), preferred_element_type=jnp.float32
    )
    token_rows = (residual + update).astype(jnp.bfloat16)
    token_map = token_rows.reshape(height, width, width_d)
    keys_vals = jnp.dot(
        token_rows,
        lax.all_gather(w_kv, "col", axis=1, tiled=True),
        preferred_element_type=jnp.float32,
    ).astype(jnp.bfloat16)
    w_full = lax.all_gather(w_o, "col", axis=1, tiled=True)
    key_heads = keys_vals[:, :width_d].reshape(-1, HEADS, HEAD)
    val_heads = keys_vals[:, width_d:].reshape(-1, HEADS, HEAD)
    query_heads = queries.reshape(latent_count, HEADS, HEAD)
    score_scale = 1.0 / math.sqrt(HEAD)
    group_size = math.gcd(HEADS, 4)
    max_parts, den_parts, num_parts = ([], [], [])
    for first_head in range(0, HEADS, group_size):
        scores = (
            jnp.einsum(
                "lhd,thd->lht",
                query_heads[:, first_head : first_head + group_size],
                key_heads[:, first_head : first_head + group_size],
                preferred_element_type=jnp.float32,
            )
            * score_scale
        )
        local_max = jnp.max(scores, axis=-1)
        weights = jnp.exp(scores - local_max[..., None])
        den_parts.append(jnp.sum(weights, axis=-1))
        max_parts.append(local_max)
        num_parts.append(
            jnp.einsum(
                "lht,thd->lhd",
                weights.astype(jnp.bfloat16),
                val_heads[:, first_head : first_head + group_size],
                preferred_element_type=jnp.float32,
            )
        )
    maxima = jnp.concatenate(max_parts, axis=1)
    denom = jnp.concatenate(den_parts, axis=1)
    numer = jnp.concatenate(num_parts, axis=1)
    peak = lax.pmax(maxima, ("row", "col"))
    factor = jnp.exp(maxima - peak)
    den_terms = denom * factor
    num_terms = (numer * factor[..., None]).reshape(latent_count, width_d)
    den_part, num_part = (
        lax.psum_scatter(den_terms, "col", scatter_dimension=0, tiled=True),
        lax.psum_scatter(num_terms, "col", scatter_dimension=0, tiled=True),
    )
    den_share, num_share = lax.psum((den_part, num_part), "row")
    own_rows = finish_latents(
        num_share.reshape(num_share.shape[0], HEADS, HEAD), den_share, latent_gain, w_full
    )
    latents = lax.all_gather(own_rows, "col", axis=0, tiled=True)
    return (token_map, latents)


def solution(mesh):
    in_specs = (
        P("row", "col", None),
        P(),
        P(),
        P(),
        P(None, "col"),
        P("col", None),
        P(None, "col"),
        P(),
        P(),
        P(None, "col"),
    )
    out_specs = (P("row", "col", None), P())
    return jax.shard_map(kernel_body, mesh=mesh, in_specs=in_specs, out_specs=out_specs, check_vma=False)
```

```python
import functools
import math

import jax
import jax.numpy as jnp
from jax import lax
from jax.experimental import pallas as pl
from jax.experimental.pallas import tpu as pltpu
from jax.sharding import PartitionSpec as P

HEADS = 12
HEAD = 64
HALO = 3
EDGE = 8
LANES = 128
MESH = pl.DeviceIdType.MESH
VMEM_BYTES = 60 * 1024 * 1024


CONV_PARTS = 8
LAG_B = 2
LAG_C = 4


def block_kernel(
    rows,
    cols,
    tokens_in,
    dw_in,
    gain,
    shift,
    w_in,
    w_out,
    w_kv,
    w_o,
    queries_in,
    latent_gain,
    tok_out,
    lat,
    tokens,
    dw,
    queries,
    g_in,
    g_out,
    g_kv,
    g_o,
    pad,
    mixed,
    normed,
    hidden,
    acc,
    tok_map,
    tok_bf,
    kv,
    h_rows,
    h_cols,
    h_corners,
    num,
    stat,
    got,
    att,
    halo_send,
    halo_recv,
    z_send,
    z_recv,
    hop_send,
    hop_recv,
    tok_send,
    tok_recv,
    sum_send,
    sum_recv,
    out_send,
    out_recv,
    local_sem,
):
    row, col = lax.axis_index("row"), lax.axis_index("col")
    height, width, depth = tokens.shape
    count = height * width
    y, x, core = row // 4, (row // 2) % 2, row % 2
    chip = row // 2
    half = depth // 2
    x_row = row + 2 * (1 - 2 * x)
    y_row = row + 4 * (1 - 2 * y)
    d_row = row + 2 * (1 - 2 * x) + 4 * (1 - 2 * y)
    mate = row + 1 - 2 * core

    barrier = pltpu.get_barrier_semaphore()
    for i in range(rows):
        for j in range(cols):
            if i or j:
                pl.semaphore_signal(
                    barrier,
                    inc=1,
                    device_id=((row + i) % rows, (col + j) % cols),
                    device_id_type=MESH,
                )

    def remote(src, dst, send, recv, device):
        return pltpu.make_async_remote_copy(
            src_ref=src,
            dst_ref=dst,
            send_sem=send,
            recv_sem=recv,
            device_id=device,
            device_id_type=MESH,
        )

    def local(src, dst, i):
        return pltpu.make_async_copy(src, dst, local_sem.at[i])

    core_lanes = pl.ds(pl.multiple_of(core * half, LANES), half)
    tokens_copy = local(tokens_in, tokens, 0)
    dw_copy = local(dw_in, dw, 1)
    queries_copy = local(queries_in.at[:, core_lanes], queries, 2)
    in_copy = local(w_in, g_in.at[col], 3)
    out_copy = local(w_out, g_out.at[col], 4)
    kv_copy = local(w_kv, g_kv.at[col // 2], 5)
    o_copy = local(w_o, g_o.at[col % 2], 6)
    for copy in (tokens_copy, dw_copy, queries_copy, in_copy, out_copy):
        copy.start()

    @pl.when(col % 2 == core)
    def _():
        kv_copy.start()

    @pl.when(col // 2 == core)
    def _():
        o_copy.start()

    both = jnp.minimum(col, cols - 1 - col)
    longer = jnp.where(cols - 1 - col > col, 1, -1)
    blocks = []
    for k in range(cols - 1):
        paired = k < 2 * both
        side = jnp.where(paired, 1 - 2 * (k % 2), longer)
        gap = jnp.where(paired, k // 2 + 1, k - both + 1)
        blocks.append(col + side * gap)

    halo = []
    for dr in (-1, 0, 1):
        for dc in (-1, 0, 1):
            if dr == 0 and dc == 0:
                continue
            cond = None
            for d, pos, n in ((dr, row, rows), (dc, col, cols)):
                if d:
                    one = (pos + d >= 0) & (pos + d < n)
                    cond = one if cond is None else cond & one
            halo.append((dr, dc, cond))

    def halo_slot(dr, dc):
        if dc == 0:
            return h_rows.at[0 if dr < 0 else 1]
        if dr == 0:
            return h_cols.at[0 if dc < 0 else 1]
        return h_corners.at[(0 if dr < 0 else 2) + (0 if dc < 0 else 1)]

    def halo_copy(i, dr, dc):
        r_span = {-1: pl.ds(0, HALO), 0: slice(None), 1: pl.ds(height - HALO, HALO)}[dr]
        c_span = {-1: pl.ds(0, EDGE), 0: slice(None), 1: pl.ds(width - EDGE, EDGE)}[dc]
        return remote(
            tokens.at[r_span, c_span],
            halo_slot(-dr, -dc),
            halo_send.at[i],
            halo_recv.at[len(halo) - 1 - i],
            (row + dr, col + dc),
        )

    def own_unit(part):
        if part < 4:
            w = (w_in, w_out)[part // 2]
            return w.at[y, x, core, part % 2], (g_in, g_out)[part // 2].at[col, y, x, core, part % 2]
        if part < 6:
            return w_kv.at[y, x, part - 4], g_kv.at[col // 2, y, x, part - 4]
        return w_o.at[y, x], g_o.at[col % 2, y, x]

    def z_id(block, part):
        if part < 4:
            return block * 4 + part
        if part < 6:
            return 4 * cols + (block // 2) * 2 + part - 4
        return 4 * cols + 4 + block % 2

    ff_jobs = 4 * (cols - 1)

    def z_copy(part, side):
        src, dst = own_unit(part)
        at = part * 2 + (0 if side > 0 else 1)
        return remote(src, dst, z_send.at[at], z_recv.at[z_id(col, part)], (row, col + side))

    def z_given(part, side, act):
        cond = (col + side >= 0) & (col + side < cols)
        if part >= 4:
            cond = cond & ((col % 2 if part < 6 else col // 2) == core)

        @pl.when(cond)
        def _():
            act(z_copy(part, side))

    def z_start(part):
        for side in (-1, 1):
            z_given(part, side, lambda c: c.start())

    def z_wait():
        for part in range(7):
            for side in (-1, 1):
                z_given(part, side, lambda c: c.wait_send())

    near = jnp.where(col < cols // 2, core, core + 2)
    far = jnp.where(col < cols // 2, core + 2, core)
    jobs = [(blocks[k], p) for k in range(cols - 1) for p in range(4)]
    jobs += [(near, 4), (near, 5), (far, 4), (far, 5)]
    jobs += [(core * 2, 6), (core * 2 + 1, 6)]

    def unit(j, dy, dx):
        block, part = jobs[j]
        yy, xx = (1 - y if dy else y), (1 - x if dx else x)
        if part < 4:
            return (g_in, g_out)[part // 2].at[block, yy, xx, core, part % 2]
        if part < 6:
            return g_kv.at[block // 2, yy, xx, part - 4]
        return g_o.at[block % 2, yy, xx]

    def turn(j):
        part = jobs[j][1]
        return j % 2 if part == 6 else part % 2

    def hop(j, leg):
        at = j * 4 + leg
        if leg == 3:
            block, part = jobs[j]
            ref = (g_in, g_out)[part // 2].at[block, :, :, core, part % 2]
            device = mate
        elif leg == 2:
            ref = unit(j, 0, 1) if turn(j) == 0 else unit(j, 1, 0)
            device = y_row if turn(j) == 0 else x_row
        else:
            ref = unit(j, 0, 0)
            device = x_row if leg == 0 else y_row
        return remote(ref, ref, hop_send.at[at], hop_recv.at[at], (device, col))

    def landed(j, leg):
        at = j * 4 + leg
        if leg == 3:
            block, part = jobs[j]
            ref = (g_in, g_out)[part // 2].at[block, :, :, 1 - core, part % 2]
        elif leg == 2:
            ref = unit(j, 1, 1)
        else:
            ref = unit(j, 0, 1) if leg == 0 else unit(j, 1, 0)
        return remote(ref, ref, hop_send.at[at], hop_recv.at[at], (mate, col))

    def onward(j):
        block = jobs[j][0]
        nxt = col + jnp.where(col > block, 1, -1)
        return (block != col) & (nxt >= 0) & (nxt < cols), nxt

    def z_arrival(j):
        block, part = jobs[j]
        ref = unit(j, 0, 0)
        return remote(ref, ref, z_send.at[0], z_recv.at[z_id(block, part)], (mate, col))

    def z_pass(j, nxt):
        block, part = jobs[j]
        ref = unit(j, 0, 0)
        return remote(ref, ref, z_send.at[14 + j], z_recv.at[z_id(block, part)], (row, nxt))

    def step_z(j, gap=None):
        cond, nxt = onward(j)
        if gap is not None:
            block = jobs[j][0]
            cond = cond & (jnp.where(col > block, col - block, block - col) == gap)

        @pl.when(cond)
        def _():
            z_arrival(j).wait_recv()
            z_pass(j, nxt).start()

    def given(j, act):
        if j < ff_jobs:
            act()
        else:
            pl.when(jobs[j][0] != col)(act)

    def step_a(j):
        @pl.when(jnp.logical_not(onward(j)[0]))
        def _():
            z_arrival(j).wait_recv()

        hop(j, 0).start()
        hop(j, 1).start()

    def step_b(j):
        landed(j, turn(j)).wait_recv()
        hop(j, 2).start()

    def step_c(j):
        landed(j, 1 - turn(j)).wait_recv()
        landed(j, 2).wait_recv()
        if j < ff_jobs:
            hop(j, 3).start()

    z_starts = {2: 0, 3: 1, 4: 4, 5: 5, 6: 9}
    passes = [(4 * r + p, p + (0, 1, 3)[r], None) for r in range(cols - 1) for p in range(4)]
    passes += [(ff_jobs, 8, None), (ff_jobs + 1, 9, None), (ff_jobs + 2, 10, None), (ff_jobs + 3, 11, None)]
    passes += [(ff_jobs + 4 + i, 12 + 2 * d, d + 1) for i in range(2) for d in range(2)]

    def z_tick(t):
        for part, at in z_starts.items():
            if at == t:
                z_start(part)
        for j, at, gap in passes:
            if at == t:
                step_z(j, gap)

    state = {"tick": 0}

    def tick():
        t = state["tick"]
        if t >= len(jobs) + LAG_C:
            return
        state["tick"] = t + 1
        z_tick(t)
        for step, lag in ((step_a, 0), (step_b, LAG_B), (step_c, LAG_C)):
            j = t - lag
            if 0 <= j < len(jobs):
                given(j, functools.partial(step, j))

    def finish(j):
        while state["tick"] <= j + LAG_C:
            tick()
        if j < ff_jobs:
            landed(j, 3).wait_recv()

    tokens_copy.wait()
    pad[pl.ds(HALO, height), pl.ds(EDGE, width), :] = tokens[...].astype(jnp.float32)
    pl.semaphore_wait(barrier, rows * cols - 1)

    z_start(0)
    for i, (dr, dc, cond) in enumerate(halo):

        @pl.when(cond)
        def _():
            halo_copy(i, dr, dc).start()

    z_start(1)
    tick()

    spans = {-1: (0, HALO), 0: (HALO, height), 1: (HALO + height, HALO)}
    lanes_of = {-1: (0, EDGE), 0: (EDGE, width), 1: (EDGE + width, EDGE)}
    for i, (dr, dc, cond) in enumerate(halo):
        r0, rn = spans[dr]
        c0, cn = lanes_of[dc]

        @pl.when(cond)
        def _():
            halo_copy(len(halo) - 1 - i, -dr, -dc).wait_recv()
            pad[pl.ds(r0, rn), pl.ds(c0, cn), :] = halo_slot(dr, dc)[...].astype(jnp.float32)

        @pl.when(jnp.logical_not(cond))
        def _():
            pad[pl.ds(r0, rn), pl.ds(c0, cn), :] = jnp.zeros((rn, cn, depth), jnp.float32)

    taps = 2 * HALO + 1
    chunks = depth // LANES
    dw_copy.wait()

    def conv_rows(first, n_rows):
        def one(step, carry):
            i = first + step // chunks
            q = pl.multiple_of((step % chunks) * LANES, LANES)
            sums = [None] * taps
            for a in range(taps):
                line = pad[i + a, :, pl.ds(q, LANES)]
                for b in range(taps):
                    lo = 0 if b < HALO else EDGE
                    hi = EDGE + width + (EDGE if b > HALO else 0)
                    term = line[lo:hi] * dw[a, pl.ds(b, 1), pl.ds(q, LANES)]
                    sums[b] = term if sums[b] is None else sums[b] + term
            total = sums[HALO]
            for b in range(taps):
                if b == HALO:
                    continue
                size = width + EDGE
                offset = EDGE - HALO + b - (0 if b < HALO else EDGE)
                total = total + pltpu.roll(sums[b], (size - offset) % size, 0)[:width]
            mixed[i, :, pl.ds(q, LANES)] = total
            return carry

        lax.fori_loop(0, n_rows * chunks, one, 0)

    group = 2
    span = group * width

    def norm_rows(g, carry):
        value = mixed[pl.ds(g * group, group), :, :].reshape(span, depth)
        center = value - jnp.mean(value, axis=-1, keepdims=True)
        spread = jnp.mean(center * center, axis=-1, keepdims=True)
        out = center * lax.rsqrt(spread + 1e-06) * gain[...][None, :] + shift[...][None, :]
        normed[pl.ds(pl.multiple_of(g * span, 16), span), :] = out.astype(jnp.bfloat16)
        return carry

    tick()
    parts = CONV_PARTS
    for part in range(parts):
        conv_rows(part * (height // parts), height // parts)
        tick()
    half_groups = height // group // 2
    lax.fori_loop(0, half_groups, norm_rows, 0)
    tick()
    lax.fori_loop(half_groups, 2 * half_groups, norm_rows, 0)
    tick()
    in_copy.wait()
    out_copy.wait()

    def wide(ref, block, lo, size):
        value = ref[(block,) + (slice(None),) * (len(ref.shape) - 2) + (pl.ds(lo, size),)]
        return value.reshape(-1, size)

    f_width = w_in.shape[-1]
    tile = 256 if f_width % 256 == 0 else LANES

    def expand(block):
        def one(n, carry):
            lo = pl.multiple_of(n * tile, tile)
            u = jnp.dot(normed[...], wide(g_in, block, lo, tile), preferred_element_type=jnp.float32)
            hidden[:, pl.ds(lo, tile)] = jax.nn.gelu(u).astype(jnp.bfloat16)
            return carry

        lax.fori_loop(0, f_width // tile, one, 0)

    def contract(block, fresh):
        def one(n, carry):
            lo = pl.multiple_of(n * 256, 256)
            part = jnp.dot(
                hidden[...], wide(g_out, block, lo, 256), preferred_element_type=jnp.float32
            )
            if fresh:
                acc[:, pl.ds(lo, 256)] = part
            else:
                acc[:, pl.ds(lo, 256)] += part
            return carry

        lax.fori_loop(0, depth // 256, one, 0)

    expand(col)
    tick()
    contract(col, True)
    tick()
    for k in range(cols - 1):
        finish(4 * k)
        finish(4 * k + 1)
        expand(blocks[k])
        finish(4 * k + 2)
        finish(4 * k + 3)
        contract(blocks[k], False)

    def close_rows(g, carry):
        base = pad[pl.ds(HALO + g * group, group), pl.ds(EDGE, width), :].reshape(span, depth)
        at = pl.ds(pl.multiple_of(g * span, 16), span)
        total = base + acc[at, :]
        tok_map[pl.ds(g * group, group), :, :] = total.reshape(group, width, depth).astype(jnp.bfloat16)
        tok_bf[0, at, :] = total.astype(jnp.bfloat16)
        return carry

    pieces = 2
    piece = count // pieces

    def tok_copy(n):
        at = pl.ds(n * piece, piece)
        return remote(tok_bf.at[0, at], tok_bf.at[1, at], tok_send.at[n], tok_recv.at[n], (mate, col))

    for n in range(pieces):
        lax.fori_loop(n * (height // group // pieces), (n + 1) * (height // group // pieces), close_rows, 0)
        tok_copy(n).start()
    tok_out_copy = local(tok_map, tok_out, 7)
    tok_out_copy.start()

    kv_width = w_kv.shape[-1]

    def project(block, side):
        def one(n, carry):
            lo = pl.multiple_of(n * LANES, LANES)
            out = jnp.dot(
                tok_bf[side], wide(g_kv, block // 2, lo, LANES), preferred_element_type=jnp.float32
            )
            kv[block // 2, pl.ds(side * count, count), pl.ds(lo, LANES)] = out.astype(jnp.bfloat16)
            return carry

        lax.fori_loop(0, kv_width // LANES, one, 0)

    @pl.when(col % 2 == core)
    def _():
        kv_copy.wait()

    finish(ff_jobs)
    finish(ff_jobs + 1)
    project(near, 0)
    for n in range(pieces):
        tok_copy(n).wait_recv()
    project(near, 1)
    finish(ff_jobs + 2)
    finish(ff_jobs + 3)
    for side in range(2):
        project(far, side)
    queries_copy.wait()

    latents = queries.shape[0]
    scale = 1.0 / math.sqrt(HEAD)
    lane = lax.broadcasted_iota(jnp.int32, (1, LANES), 1)
    pairs = half // LANES
    stat_lanes = pl.ds(half, LANES)
    step_rows = latents // 2
    share = latents // (rows // 2 * cols)

    def attend(pair):
        lanes = pl.ds(pair * LANES, LANES)

        def one(n, carry):
            at = pl.ds(pl.multiple_of(n * step_rows, 16), step_rows)
            q = queries[at, lanes]
            keys = kv[0, :, lanes]
            vals = kv[1, :, lanes]
            base = jnp.zeros((step_rows, LANES), jnp.float32) if pair == 0 else stat[at, :]
            outs = []
            for s in range(2):
                keep = (lane // HEAD) == s
                q_one = jnp.where(keep, q, jnp.zeros_like(q))
                scores = lax.dot_general(
                    q_one, keys, (((1,), (1,)), ((), ())), preferred_element_type=jnp.float32
                )
                top = jnp.max(scores, axis=-1, keepdims=True)
                weights = jnp.exp((scores - top) * scale)
                den = jnp.sum(weights, axis=-1, keepdims=True)
                outs.append(
                    jnp.dot(weights.astype(jnp.bfloat16), vals, preferred_element_type=jnp.float32)
                )
                base = jnp.where(lane == pair * 2 + s, top * scale, base)
                base = jnp.where(lane == pair * 2 + s + 8, den, base)
            num[at, lanes] = jnp.where(lane < HEAD, outs[0], outs[1]).astype(jnp.bfloat16)
            if pair < pairs - 1:
                stat[at, :] = base
            else:
                high = base.astype(jnp.bfloat16).astype(jnp.float32)
                rest = base - high
                mid = rest.astype(jnp.bfloat16).astype(jnp.float32)
                low = rest - mid
                out = high + pltpu.roll(mid, 16, 1) + pltpu.roll(low, 32, 1)
                num[at, stat_lanes] = out.astype(jnp.bfloat16)
            return carry

        lax.fori_loop(0, latents // step_rows, one, 0)

    peers = [(i, j) for i in range(rows // 2) for j in range(cols) if i or j]

    def sum_copy(i, j, part):
        to_chip, to_col = (chip + i) % (rows // 2), (col + j) % cols
        slot = i * cols + j
        give = pl.ds(pl.multiple_of((to_chip * cols + to_col) * share, 16), share)
        size = LANES if part < pairs - 1 else 2 * LANES
        lanes = pl.ds(part * LANES, size)
        at = slot * pairs + part
        return remote(
            num.at[give, lanes],
            got.at[slot, :, lanes],
            sum_send.at[at],
            sum_recv.at[at],
            (to_chip * 2 + core, to_col),
        )

    for pair in range(pairs):
        attend(pair)
        for i, j in peers:
            sum_copy(i, j, pair).start()
        if pair == 0:
            while state["tick"] < len(jobs) + LAG_C:
                tick()

    for i, (dr, dc, cond) in enumerate(halo):

        @pl.when(cond)
        def _():
            halo_copy(i, dr, dc).wait_send()

    z_wait()

    def sent(j):
        for leg in range(4 if j < ff_jobs else 3):
            hop(j, leg).wait_send()
        cond, nxt = onward(j)

        @pl.when(cond)
        def _():
            z_pass(j, nxt).wait_send()

    for j in range(len(jobs)):
        given(j, functools.partial(sent, j))
    for n in range(pieces):
        tok_copy(n).wait_send()
    tok_out_copy.wait()

    @pl.when(col // 2 == core)
    def _():
        o_copy.wait()

    def own_rows(at_chip, at_col):
        return pl.ds(pl.multiple_of((at_chip * cols + at_col) * share, 16), share)

    def spread(factor):
        parts = []
        for pair in range(pairs):
            lo = jnp.broadcast_to(factor[:, 2 * pair : 2 * pair + 1], (share, LANES))
            hi = jnp.broadcast_to(factor[:, 2 * pair + 1 : 2 * pair + 2], (share, LANES))
            parts.append(jnp.where(lane < HEAD, lo, hi))
        return jnp.concatenate(parts, axis=-1)

    for i, j in peers:
        for part in range(pairs):
            sum_copy(i, j, part).wait_recv()
    mine = own_rows(chip, col)
    slots = [None] + [i * cols + j for i, j in peers]

    def source(slot, lanes):
        value = num[mine, lanes] if slot is None else got[slot, :, lanes]
        return value.astype(jnp.float32)

    stats = []
    for slot in slots:
        s = source(slot, stat_lanes)
        stats.append(s + (pltpu.roll(s, LANES - 16, 1) + pltpu.roll(s, LANES - 32, 1)))
    peak = functools.reduce(jnp.maximum, stats)
    den, total = None, None
    for slot, s in zip(slots, stats):
        factor = jnp.exp(s - peak)
        d = pltpu.roll(s, LANES - 8, 1) * factor
        t = source(slot, pl.ds(0, half)) * spread(factor)
        den = d if den is None else den + d
        total = t if total is None else total + t
    att[core] = total / spread(den)
    n_sum = len(slots) * pairs
    swap = remote(att.at[core], att.at[core], sum_send.at[n_sum], sum_recv.at[n_sum], (mate, col))
    swap.start()
    for i, j in peers:
        for part in range(pairs):
            sum_copy(i, j, part).wait_send()
    remote(
        att.at[1 - core], att.at[1 - core], sum_send.at[n_sum], sum_recv.at[n_sum], (mate, col)
    ).wait_recv()
    first, second = att[0], att[1]
    squares = (
        jnp.sum(first * first, axis=-1, keepdims=True)
        + jnp.sum(second * second, axis=-1, keepdims=True)
    ) / depth
    inverse = lax.rsqrt(squares + 1e-06)
    scaled = jnp.concatenate([first, second], axis=-1) * inverse * latent_gain[...][None, :]
    turned = g_o[...].reshape(half, depth)
    done = lax.dot_general(
        scaled.astype(jnp.bfloat16), turned, (((1,), (1,)), ((), ())), preferred_element_type=jnp.float32
    )
    lat[mine, core_lanes] = done.astype(jnp.bfloat16)

    planes = [col] + blocks
    chips = [chip, x_row // 2, y_row // 2, d_row // 2]
    ways = [x_row, y_row, d_row]

    def out_copy_z(k):
        ref = lat.at[mine, core_lanes]
        return remote(ref, ref, out_send.at[k], out_recv.at[col], (row, blocks[k]))

    base_p, base_c = cols, cols + 3 * cols

    def out_copy_plane(n, way):
        ref = lat.at[own_rows(chip, planes[n]), core_lanes]
        at = base_p + n * 3 + way
        return remote(ref, ref, out_send.at[at], out_recv.at[at], (ways[way], col))

    def out_landed_plane(n, way):
        ref = lat.at[own_rows(chips[way + 1], planes[n]), core_lanes]
        at = base_p + n * 3 + way
        return remote(ref, ref, out_send.at[at], out_recv.at[at], (mate, col))

    mate_lanes = pl.ds(pl.multiple_of((1 - core) * half, LANES), half)

    def out_copy_core(n, who, lanes):
        ref = lat.at[own_rows(chips[who], planes[n]), lanes]
        at = base_c + n * 4 + who
        return remote(ref, ref, out_send.at[at], out_recv.at[at], (mate, col))

    def fan(n):
        for way in range(3):
            out_copy_plane(n, way).start()
        out_copy_core(n, 0, core_lanes).start()

    for k in range(cols - 1):
        out_copy_z(k).start()
    fan(0)
    for k in range(cols - 1):
        ref = lat.at[own_rows(chip, blocks[k]), core_lanes]
        remote(ref, ref, out_send.at[0], out_recv.at[blocks[k]], (mate, col)).wait_recv()
        fan(k + 1)
    for n in range(cols):
        for way in range(3):
            out_landed_plane(n, way).wait_recv()
            out_copy_core(n, way + 1, core_lanes).start()
    swap.wait_send()
    for k in range(cols - 1):
        out_copy_z(k).wait_send()
    for n in range(cols):
        for way in range(3):
            out_copy_plane(n, way).wait_send()
    for n in range(cols):
        for who in range(4):
            out_copy_core(n, who, mate_lanes).wait_recv()
            out_copy_core(n, who, core_lanes).wait_send()


def hbm(n):
    return [pl.BlockSpec(memory_space=pl.ANY)] * n


def vmem(n):
    return [pl.BlockSpec(memory_space=pltpu.VMEM)] * n


def fits(mesh_rows, mesh_cols, tokens, w_in, w_out, w_kv, queries, w_o):
    height, width, depth = tokens.shape
    return (
        mesh_rows == 8
        and mesh_cols == 4
        and depth == HEADS * HEAD
        and depth % 256 == 0
        and depth % (2 * LANES) == 0
        and w_in.shape[1] % LANES == 0
        and w_out.shape[0] % (32 * mesh_rows) == 0
        and depth % (32 * mesh_rows) == 0
        and w_kv.shape[1] * 2 == depth
        and w_o.shape[1] % 64 == 0
        and w_o.shape[1] * mesh_cols == depth
        and queries.shape[0] % (16 * mesh_rows // 2 * mesh_cols) == 0
        and height % 4 == 0
        and width % 8 == 0
        and height * width % 32 == 0
    )


def kernel_body(tokens, dw_kernel, norm_gain, norm_shift, w_in, w_out, w_kv, queries, latent_gain, w_o):
    rows, cols = lax.axis_size("row"), lax.axis_size("col")
    height, width, depth = tokens.shape
    if not fits(rows, cols, tokens, w_in, w_out, w_kv, queries, w_o):
        return body(
            tokens, dw_kernel, norm_gain, norm_shift, w_in, w_out, w_kv, queries, latent_gain, w_o
        )
    count = height * width
    latents = queries.shape[0]
    f_width = w_in.shape[1]
    half = depth // 2
    bf16, f32 = jnp.bfloat16, jnp.float32

    def cut(w, lead):
        size = w.shape[0]
        for n in lead:
            size //= n
        return w.reshape(lead + (size, w.shape[1]))

    shards = [
        cut(w_in, (2, 2, 2, 2)),
        cut(w_out, (2, 2, 2, 2)),
        cut(w_kv, (2, 2, 2)),
        cut(w_o.T, (2, 2)),
    ]
    share = latents // (rows // 2 * cols)
    pairs = half // LANES
    n_jobs = 4 * (cols - 1) + 4 + 2
    n_sum = rows // 2 * cols * pairs + 1
    n_out = cols + 3 * cols + 4 * cols
    dma = pltpu.SemaphoreType.DMA
    return pl.pallas_call(
        functools.partial(block_kernel, rows, cols),
        out_shape=(
            jax.ShapeDtypeStruct(tokens.shape, bf16),
            jax.ShapeDtypeStruct((latents, depth), bf16),
        ),
        in_specs=hbm(2) + vmem(2) + hbm(5) + vmem(1),
        out_specs=(hbm(1)[0], vmem(1)[0]),
        scratch_shapes=[
            pltpu.VMEM(tokens.shape, bf16),
            pltpu.VMEM(dw_kernel.shape, f32),
            pltpu.VMEM((latents, half), bf16),
            pltpu.VMEM((cols,) + shards[0].shape, bf16),
            pltpu.VMEM((cols,) + shards[1].shape, bf16),
            pltpu.VMEM((2,) + shards[2].shape, bf16),
            pltpu.VMEM((2,) + shards[3].shape, bf16),
            pltpu.VMEM((height + 2 * HALO, width + 2 * EDGE, depth), f32),
            pltpu.VMEM((height, width, depth), f32),
            pltpu.VMEM((count, depth), bf16),
            pltpu.VMEM((count, f_width), bf16),
            pltpu.VMEM((count, depth), f32),
            pltpu.VMEM((height, width, depth), bf16),
            pltpu.VMEM((2, count, depth), bf16),
            pltpu.VMEM((2, 2 * count, half), bf16),
            pltpu.VMEM((2, HALO, width, depth), bf16),
            pltpu.VMEM((2, height, EDGE, depth), bf16),
            pltpu.VMEM((4, HALO, EDGE, depth), bf16),
            pltpu.VMEM((latents, half + LANES), bf16),
            pltpu.VMEM((latents, LANES), f32),
            pltpu.VMEM((rows // 2 * cols, share, half + LANES), bf16),
            pltpu.VMEM((2, share, half), f32),
            dma((8,)),
            dma((8,)),
            dma((14 + n_jobs,)),
            dma((4 * cols + 6,)),
            dma((n_jobs * 4,)),
            dma((n_jobs * 4,)),
            dma((2,)),
            dma((2,)),
            dma((n_sum,)),
            dma((n_sum,)),
            dma((n_out,)),
            dma((n_out,)),
            dma((8,)),
        ],
        compiler_params=pltpu.CompilerParams(
            collective_id=0, has_side_effects=True, vmem_limit_bytes=VMEM_BYTES
        ),
        name="block",
    )(
        tokens,
        dw_kernel,
        norm_gain,
        norm_shift,
        *shards,
        queries,
        latent_gain,
    )


def with_halo(cells, sides, width):
    for axis, dim in sides:
        count = lax.axis_size(axis)
        ends = count - 1
        head = lax.slice_in_dim(cells, 0, width, axis=dim)
        tail = lax.slice_in_dim(cells, cells.shape[dim] - width, cells.shape[dim], axis=dim)
        cells = jnp.concatenate(
            [
                lax.ppermute(tail, axis, [(i, (i + 1) % count) for i in range(ends)]),
                cells,
                lax.ppermute(head, axis, [((i + 1) % count, i) for i in range(ends)]),
            ],
            axis=dim,
        )
    return cells


def conv_taps(padded, height, width, dw_kernel):
    mixed = jnp.zeros((height, width, padded.shape[2]), jnp.float32)
    for row_tap in range(7):
        for col_tap in range(7):
            mixed = (
                mixed
                + padded[row_tap : row_tap + height, col_tap : col_tap + width]
                * dw_kernel[row_tap, col_tap]
            )
    return mixed


def layer_norm(mixed, norm_gain, norm_shift):
    center = mixed - jnp.mean(mixed, axis=-1, keepdims=True)
    spread = jnp.mean(center * center, axis=-1, keepdims=True)
    return (center * lax.rsqrt(spread + 1e-06) * norm_gain + norm_shift).astype(jnp.bfloat16)


def finish_latents(numer, denom, latent_gain, w_full):
    attended = (numer / denom[..., None]).reshape(numer.shape[0], -1)
    squares = jnp.mean(attended * attended, axis=-1, keepdims=True)
    scaled = (attended * lax.rsqrt(squares + 1e-06) * latent_gain).astype(jnp.bfloat16)
    return jnp.dot(scaled, w_full, preferred_element_type=jnp.float32).astype(jnp.bfloat16)


def body(tokens, dw_kernel, norm_gain, norm_shift, w_in, w_out, w_kv, queries, latent_gain, w_o):
    height, width, width_d = tokens.shape
    latent_count = queries.shape[0]
    padded = with_halo(tokens, (("row", 0), ("col", 1)), 3)
    mixed = conv_taps(padded.astype(jnp.float32), height, width, dw_kernel)
    normed = layer_norm(mixed, norm_gain, norm_shift).reshape(height * width, width_d)
    residual = tokens.reshape(height * width, width_d).astype(jnp.float32)
    hidden = jax.nn.gelu(
        jnp.dot(
            normed,
            lax.all_gather(w_in, "col", axis=1, tiled=True),
            preferred_element_type=jnp.float32,
        )
    ).astype(jnp.bfloat16)
    update = jnp.dot(
        hidden, lax.all_gather(w_out, "col", axis=0, tiled=True), preferred_element_type=jnp.float32
    )
    token_rows = (residual + update).astype(jnp.bfloat16)
    token_map = token_rows.reshape(height, width, width_d)
    keys_vals = jnp.dot(
        token_rows,
        lax.all_gather(w_kv, "col", axis=1, tiled=True),
        preferred_element_type=jnp.float32,
    ).astype(jnp.bfloat16)
    w_full = lax.all_gather(w_o, "col", axis=1, tiled=True)
    key_heads = keys_vals[:, :width_d].reshape(-1, HEADS, HEAD)
    val_heads = keys_vals[:, width_d:].reshape(-1, HEADS, HEAD)
    query_heads = queries.reshape(latent_count, HEADS, HEAD)
    score_scale = 1.0 / math.sqrt(HEAD)
    group_size = math.gcd(HEADS, 4)
    max_parts, den_parts, num_parts = ([], [], [])
    for first_head in range(0, HEADS, group_size):
        scores = (
            jnp.einsum(
                "lhd,thd->lht",
                query_heads[:, first_head : first_head + group_size],
                key_heads[:, first_head : first_head + group_size],
                preferred_element_type=jnp.float32,
            )
            * score_scale
        )
        local_max = jnp.max(scores, axis=-1)
        weights = jnp.exp(scores - local_max[..., None])
        den_parts.append(jnp.sum(weights, axis=-1))
        max_parts.append(local_max)
        num_parts.append(
            jnp.einsum(
                "lht,thd->lhd",
                weights.astype(jnp.bfloat16),
                val_heads[:, first_head : first_head + group_size],
                preferred_element_type=jnp.float32,
            )
        )
    maxima = jnp.concatenate(max_parts, axis=1)
    denom = jnp.concatenate(den_parts, axis=1)
    numer = jnp.concatenate(num_parts, axis=1)
    peak = lax.pmax(maxima, ("row", "col"))
    factor = jnp.exp(maxima - peak)
    den_terms = denom * factor
    num_terms = (numer * factor[..., None]).reshape(latent_count, width_d)
    den_part, num_part = (
        lax.psum_scatter(den_terms, "col", scatter_dimension=0, tiled=True),
        lax.psum_scatter(num_terms, "col", scatter_dimension=0, tiled=True),
    )
    den_share, num_share = lax.psum((den_part, num_part), "row")
    own_rows = finish_latents(
        num_share.reshape(num_share.shape[0], HEADS, HEAD), den_share, latent_gain, w_full
    )
    latents = lax.all_gather(own_rows, "col", axis=0, tiled=True)
    return (token_map, latents)


def solution(mesh):
    in_specs = (
        P("row", "col", None),
        P(),
        P(),
        P(),
        P(None, "col"),
        P("col", None),
        P(None, "col"),
        P(),
        P(),
        P(None, "col"),
    )
    out_specs = (P("row", "col", None), P())
    return jax.shard_map(kernel_body, mesh=mesh, in_specs=in_specs, out_specs=out_specs, check_vma=False)
```

```python
import functools
import math

import jax
import jax.numpy as jnp
from jax import lax
from jax.experimental import pallas as pl
from jax.experimental.pallas import tpu as pltpu
from jax.sharding import PartitionSpec as P

HEADS = 12
HEAD = 64
HALO = 3
LOG2E = math.log2(math.e)
EDGE = 8
LANES = 128
MESH = pl.DeviceIdType.MESH
VMEM_BYTES = 60 * 1024 * 1024


CONV_PARTS = 4
WIDE = (3, 4, 5)
HALO_AFTER = 4
PRE = 3
Z_LAST = 19
LAG_B = 2
LAG_C = 4


def block_kernel(
    rows,
    cols,
    tokens_in,
    dw_in,
    gain,
    shift,
    w_in,
    w_out,
    w_kv,
    w_o,
    queries_in,
    latent_gain,
    tok_out,
    lat,
    tokens,
    dw,
    queries,
    g_in,
    g_out,
    g_kv,
    g_o,
    pad,
    mixed,
    normed,
    hidden,
    acc,
    tok_map,
    tok_bf,
    kv,
    h_rows,
    h_cols,
    col_out,
    h_corners,
    num,
    stat,
    got,
    att,
    halo_send,
    halo_recv,
    z_send,
    z_recv,
    hop_send,
    hop_recv,
    tok_send,
    tok_recv,
    sum_send,
    sum_recv,
    out_send,
    out_recv,
    local_sem,
):
    row, col = lax.axis_index("row"), lax.axis_index("col")
    height, width, depth = tokens.shape
    count = height * width
    y, x, core = row // 4, (row // 2) % 2, row % 2
    chip = row // 2
    half = depth // 2
    x_row = row + 2 * (1 - 2 * x)
    y_row = row + 4 * (1 - 2 * y)
    d_row = row + 2 * (1 - 2 * x) + 4 * (1 - 2 * y)
    mate = row + 1 - 2 * core

    def remote(src, dst, send, recv, device):
        return pltpu.make_async_remote_copy(
            src_ref=src,
            dst_ref=dst,
            send_sem=send,
            recv_sem=recv,
            device_id=device,
            device_id_type=MESH,
        )

    def local(src, dst, i):
        return pltpu.make_async_copy(src, dst, local_sem.at[i])

    core_lanes = pl.ds(pl.multiple_of(core * half, LANES), half)
    tokens_copy = local(tokens_in, tokens, 0)
    dw_copy = local(dw_in, dw, 1)
    queries_copy = local(queries_in.at[:, core_lanes], queries, 2)
    in_copy = local(w_in, g_in.at[col], 3)
    out_copy = local(w_out, g_out.at[col], 4)
    kv_copy = local(w_kv, g_kv.at[col // 2], 5)
    o_copy = local(w_o, g_o.at[col % 2], 6)
    for copy in (tokens_copy, dw_copy, queries_copy, in_copy, out_copy):
        copy.start()

    @pl.when(col % 2 == core)
    def _():
        kv_copy.start()

    @pl.when(col // 2 == core)
    def _():
        o_copy.start()

    both = jnp.minimum(col, cols - 1 - col)
    longer = jnp.where(cols - 1 - col > col, 1, -1)
    blocks = []
    for k in range(cols - 1):
        paired = k < 2 * both
        side = jnp.where(paired, 1 - 2 * (k % 2), longer)
        gap = jnp.where(paired, k // 2 + 1, k - both + 1)
        blocks.append(col + side * gap)

    halo = []
    for dr in (-1, 0, 1):
        for dc in (-1, 0, 1):
            if dr == 0 and dc == 0:
                continue
            cond = None
            for d, pos, n in ((dr, row, rows), (dc, col, cols)):
                if d:
                    one = (pos + d >= 0) & (pos + d < n)
                    cond = one if cond is None else cond & one
            halo.append((dr, dc, cond))

    barrier = pltpu.get_barrier_semaphore()
    peers = [(None, (x_row, col)), (None, (y_row, col)), (None, (mate, col))]
    for dr, dc, cond in halo:
        if dc == 0:
            cond = cond & (row + dr != mate) & (row + dr != x_row) & (row + dr != y_row)
        peers.append((cond, (row + dr, col + dc)))
    greeted = 0
    for cond, device in peers:
        if cond is None:
            pl.semaphore_signal(barrier, inc=1, device_id=device, device_id_type=MESH)
            greeted = greeted + 1
        else:

            @pl.when(cond)
            def _():
                pl.semaphore_signal(barrier, inc=1, device_id=device, device_id_type=MESH)

            greeted = greeted + jnp.where(cond, 1, 0)

    def halo_slot(dr, dc):
        if dc == 0:
            return h_rows.at[0 if dr < 0 else 1]
        if dr == 0:
            return h_cols.at[0 if dc < 0 else 1]
        return h_corners.at[(0 if dr < 0 else 2) + (0 if dc < 0 else 1)]

    def halo_copy(i, dr, dc):
        r_span = {-1: pl.ds(0, HALO), 0: slice(None), 1: pl.ds(height - HALO, HALO)}[dr]
        c_span = {-1: pl.ds(0, EDGE), 0: slice(None), 1: pl.ds(width - EDGE, EDGE)}[dc]
        return remote(
            tokens.at[r_span, c_span] if dr or not dc else col_out.at[0 if dc < 0 else 1],
            halo_slot(-dr, -dc),
            halo_send.at[i],
            halo_recv.at[len(halo) - 1 - i],
            (row + dr, col + dc),
        )

    def own_unit(part, across=False):
        yy, xx = (1 - y, 1 - x) if across else (y, x)
        if part < 4:
            w = (w_in, w_out)[part // 2]
            return w.at[yy, xx, core, part % 2], (g_in, g_out)[part // 2].at[col, yy, xx, core, part % 2]
        if part < 6:
            return w_kv.at[yy, xx, part - 4], g_kv.at[col // 2, yy, xx, part - 4]
        return w_o.at[yy, xx], g_o.at[col % 2, yy, xx]

    def z_id(block, part):
        if part < 4:
            return block * 4 + part
        if part < 6:
            return 4 * cols + (block // 2) * 2 + part - 4
        return 4 * cols + 4 + block % 2

    ff_jobs = 4 * (cols - 1)
    n_send, n_recv = 14 + ff_jobs + 6, 4 * cols + 6

    def z_copies(part, side):
        made = []
        for across in (False, True) if part in WIDE else (False,):
            src, dst = own_unit(part, across)
            at = part * 2 + (0 if side > 0 else 1) + (n_send if across else 0)
            into = z_id(col, part) + (n_recv if across else 0)
            made.append(remote(src, dst, z_send.at[at], z_recv.at[into], (row, col + side)))
        return made

    def z_given(part, side, act):
        cond = (col + side >= 0) & (col + side < cols)
        if part >= 4:
            cond = cond & ((col % 2 if part < 6 else col // 2) == core)

        @pl.when(cond)
        def _():
            for c in z_copies(part, side):
                act(c)

    def z_start(part):
        for side in (-1, 1):
            z_given(part, side, lambda c: c.start())

    def z_wait():
        for part in range(7):
            for side in (-1, 1):
                z_given(part, side, lambda c: c.wait_send())

    near = jnp.where(col < cols // 2, core, core + 2)
    far = jnp.where(col < cols // 2, core + 2, core)
    jobs = [(blocks[k], p) for k in range(cols - 1) for p in range(4)]
    jobs += [(near, 4), (near, 5), (far, 4), (far, 5)]
    jobs += [(core * 2, 6), (core * 2 + 1, 6)]

    def unit(j, dy, dx):
        block, part = jobs[j]
        yy, xx = (1 - y if dy else y), (1 - x if dx else x)
        if part < 4:
            return (g_in, g_out)[part // 2].at[block, yy, xx, core, part % 2]
        if part < 6:
            return g_kv.at[block // 2, yy, xx, part - 4]
        return g_o.at[block % 2, yy, xx]

    def turn(j):
        part = jobs[j][1]
        return j % 2 if part == 6 or 3 in WIDE else part % 2

    def hop(j, leg):
        at = j * 4 + leg
        if leg == 3:
            block, part = jobs[j]
            ref = (g_in, g_out)[part // 2].at[block, :, :, core, part % 2]
            device = mate
        elif leg == 2:
            ref = unit(j, 0, 1) if turn(j) == 0 else unit(j, 1, 0)
            device = y_row if turn(j) == 0 else x_row
        else:
            ref = unit(j, 0, 0)
            device = x_row if leg == 0 else y_row
        return remote(ref, ref, hop_send.at[at], hop_recv.at[at], (device, col))

    def landed(j, leg):
        at = j * 4 + leg
        if leg == 3:
            block, part = jobs[j]
            ref = (g_in, g_out)[part // 2].at[block, :, :, 1 - core, part % 2]
        elif leg == 2:
            ref = unit(j, 1, 1)
        else:
            ref = unit(j, 0, 1) if leg == 0 else unit(j, 1, 0)
        return remote(ref, ref, hop_send.at[at], hop_recv.at[at], (mate, col))

    def onward(j):
        block = jobs[j][0]
        nxt = col + jnp.where(col > block, 1, -1)
        return (block != col) & (nxt >= 0) & (nxt < cols), nxt

    def is_wide(j):
        return jobs[j][1] in WIDE

    def z_arrival(j, across=False):
        block, part = jobs[j]
        ref = unit(j, 1, 1) if across else unit(j, 0, 0)
        at = z_id(block, part) + (n_recv if across else 0)
        return remote(ref, ref, z_send.at[0], z_recv.at[at], (mate, col))

    def z_pass(j, nxt, across=False):
        block, part = jobs[j]
        ref = unit(j, 1, 1) if across else unit(j, 0, 0)
        at = z_id(block, part) + (n_recv if across else 0)
        by = 14 + j + (n_send if across else 0)
        return remote(ref, ref, z_send.at[by], z_recv.at[at], (row, nxt))

    def step_z(j, gap=None):
        cond, nxt = onward(j)
        if gap is not None:
            block = jobs[j][0]
            cond = cond & (jnp.where(col > block, col - block, block - col) == gap)

        @pl.when(cond)
        def _():
            for across in (False, True) if is_wide(j) else (False,):
                z_arrival(j, across).wait_recv()
                z_pass(j, nxt, across).start()

    def given(j, act):
        if j < ff_jobs:
            act()
        else:
            pl.when(jobs[j][0] != col)(act)

    def step_a(j):
        @pl.when(jnp.logical_not(onward(j)[0]))
        def _():
            z_arrival(j).wait_recv()

        hop(j, 0).start()
        hop(j, 1).start()

    def step_b(j):
        if not is_wide(j):
            landed(j, turn(j)).wait_recv()
            hop(j, 2).start()

    def step_c(j):
        if is_wide(j):
            landed(j, 0).wait_recv()
            landed(j, 1).wait_recv()

            @pl.when(jnp.logical_not(onward(j)[0]))
            def _():
                z_arrival(j, True).wait_recv()

        else:
            landed(j, 1 - turn(j)).wait_recv()
            landed(j, 2).wait_recv()
        if j < ff_jobs:
            hop(j, 3).start()

    last = ff_jobs + 4
    z_starts = {p: p - 2 for p in range(max(HALO_AFTER, 2), 4)} | {4: 4, 5: 5, 6: 9}
    passes = [(4 * r + p, p + (0, 1, 3)[r], None) for r in range(cols - 1) for p in range(4)]
    passes += [(ff_jobs, 8, None), (ff_jobs + 1, 9, None), (ff_jobs + 2, 10, None), (ff_jobs + 3, 11, None)]
    passes += [(last + i, 14 + 3 * d, d + 1) for i in range(2) for d in range(2)]

    def z_tick(t):
        for part, at in z_starts.items():
            if at == t:
                z_start(part)
        for j, at, gap in passes:
            if at == t:
                step_z(j, gap)

    steps = {"z": z_tick, "a": step_a, "b": step_b, "c": step_c}
    plan = []
    for t in range(last):
        plan.append(("z", t))
        for name, lag in (("a", 0), ("b", LAG_B), ("c", LAG_C)):
            if t - lag >= 0:
                plan.append((name, t - lag))
        plan.append(("tick", t))
    for t in range(last, last + LAG_B):
        plan.append(("z", t))
        plan.append(("b", t - LAG_B))
        if t - LAG_C >= 0:
            plan.append(("c", t - LAG_C))
    for t in range(last + LAG_B, Z_LAST):
        plan.append(("z", t))
    plan += [("a", j) for j in range(last, len(jobs))]
    plan += [("c", j) for j in range(last + LAG_B - LAG_C, last)]
    plan += [("b", j) for j in range(last, len(jobs))]
    plan += [("c", j) for j in range(last, len(jobs))]

    def run():
        name, j = plan.pop(0)
        if name == "z":
            z_tick(j)
        elif name != "tick":
            given(j, functools.partial(steps[name], j))
        return name, j

    def tick():
        while plan and run()[0] != "tick":
            pass

    def until(name, j):
        while (name, j) in plan:
            run()

    def finish(j):
        until("c", j)
        if j < ff_jobs:
            landed(j, 3).wait_recv()

    tokens_copy.wait()
    pad[pl.ds(HALO, height), pl.ds(EDGE, width), :] = tokens[...].astype(jnp.float32)
    for side in range(2):
        edge = pl.ds(side * (EDGE + width), EDGE)
        pad[pl.ds(HALO, height), edge, :] = jnp.zeros((height, EDGE, depth), jnp.float32)
        for n in range(HALO):
            at = EDGE + (n if side == 0 else width - HALO + n)
            col_out[side, n] = pad[pl.ds(HALO, height), at, :].astype(jnp.bfloat16)
    pl.semaphore_wait(barrier, greeted)

    for part in range(HALO_AFTER):
        z_start(part)
    for i, (dr, dc, cond) in enumerate(halo):

        @pl.when(cond)
        def _():
            halo_copy(i, dr, dc).start()

    for part in range(HALO_AFTER, 2):
        z_start(part)
    for _ in range(PRE):
        tick()

    spans = {-1: (0, HALO), 0: (HALO, height), 1: (HALO + height, HALO)}
    lanes_of = {-1: (0, EDGE), 0: (EDGE, width), 1: (EDGE + width, EDGE)}
    for i, (dr, dc, cond) in enumerate(halo):
        r0, rn = spans[dr]
        c0, cn = lanes_of[dc]

        @pl.when(cond)
        def _():
            halo_copy(len(halo) - 1 - i, -dr, -dc).wait_recv()
            if dr == 0:
                for n in range(HALO):
                    at = EDGE - HALO + n if dc < 0 else EDGE + width + n
                    side = 0 if dc < 0 else 1
                    pad[pl.ds(HALO, height), at, :] = h_cols[side, n].astype(jnp.float32)
            else:
                pad[pl.ds(r0, rn), pl.ds(c0, cn), :] = halo_slot(dr, dc)[...].astype(jnp.float32)

        if dr:

            @pl.when(jnp.logical_not(cond))
            def _():
                pad[pl.ds(r0, rn), pl.ds(c0, cn), :] = jnp.zeros((rn, cn, depth), jnp.float32)

    taps = 2 * HALO + 1
    chunks = depth // LANES
    dw_copy.wait()

    def conv_rows(first, n_rows):
        def one(step, carry):
            i = first + step // chunks
            q = pl.multiple_of((step % chunks) * LANES, LANES)
            sums = [None] * taps
            for a in range(taps):
                line = pad[i + a, :, pl.ds(q, LANES)]
                for b in range(taps):
                    lo = 0 if b < HALO else EDGE
                    hi = EDGE + width + (EDGE if b > HALO else 0)
                    term = line[lo:hi] * dw[a, pl.ds(b, 1), pl.ds(q, LANES)]
                    sums[b] = term if sums[b] is None else sums[b] + term
            total = sums[HALO]
            for b in range(taps):
                if b == HALO:
                    continue
                size = width + EDGE
                offset = EDGE - HALO + b - (0 if b < HALO else EDGE)
                total = total + pltpu.roll(sums[b], (size - offset) % size, 0)[:width]
            mixed[i, :, pl.ds(q, LANES)] = total
            return carry

        lax.fori_loop(0, n_rows * chunks, one, 0)

    group = 2
    span = group * width

    def norm_rows(g, carry):
        value = mixed[pl.ds(g * group, group), :, :].reshape(span, depth)
        center = value - jnp.mean(value, axis=-1, keepdims=True)
        spread = jnp.mean(center * center, axis=-1, keepdims=True)
        out = center * lax.rsqrt(spread + 1e-06) * gain[...][None, :] + shift[...][None, :]
        normed[pl.ds(pl.multiple_of(g * span, 16), span), :] = out.astype(jnp.bfloat16)
        return carry

    tick()
    parts = CONV_PARTS
    for part in range(parts):
        conv_rows(part * (height // parts), height // parts)
        tick()
    half_groups = height // group // 2
    lax.fori_loop(0, half_groups, norm_rows, 0)
    tick()
    lax.fori_loop(half_groups, 2 * half_groups, norm_rows, 0)
    tick()
    in_copy.wait()
    out_copy.wait()

    def wide(ref, block, lo, size):
        value = ref[(block,) + (slice(None),) * (len(ref.shape) - 2) + (pl.ds(lo, size),)]
        return value.reshape(-1, size)

    f_width = w_in.shape[-1]
    tile = 256 if f_width % 256 == 0 else LANES

    def expand(block):
        def one(n, carry):
            lo = pl.multiple_of(n * tile, tile)
            u = jnp.dot(normed[...], wide(g_in, block, lo, tile), preferred_element_type=jnp.float32)
            hidden[:, pl.ds(lo, tile)] = jax.nn.gelu(u).astype(jnp.bfloat16)
            return carry

        lax.fori_loop(0, f_width // tile, one, 0)

    def contract(block, fresh):
        def one(n, carry):
            lo = pl.multiple_of(n * 256, 256)
            part = jnp.dot(
                hidden[...], wide(g_out, block, lo, 256), preferred_element_type=jnp.float32
            )
            if fresh:
                acc[:, pl.ds(lo, 256)] = part
            else:
                acc[:, pl.ds(lo, 256)] += part
            return carry

        lax.fori_loop(0, depth // 256, one, 0)

    expand(col)
    tick()
    contract(col, True)
    tick()
    for k in range(cols - 1):
        finish(4 * k)
        finish(4 * k + 1)
        expand(blocks[k])
        finish(4 * k + 2)
        finish(4 * k + 3)
        contract(blocks[k], False)

    def close_rows(g, carry):
        base = pad[pl.ds(HALO + g * group, group), pl.ds(EDGE, width), :].reshape(span, depth)
        at = pl.ds(pl.multiple_of(g * span, 16), span)
        total = base + acc[at, :]
        tok_map[pl.ds(g * group, group), :, :] = total.reshape(group, width, depth).astype(jnp.bfloat16)
        tok_bf[0, at, :] = total.astype(jnp.bfloat16)
        return carry

    pieces = 2
    piece = count // pieces

    def tok_copy(n):
        at = pl.ds(n * piece, piece)
        return remote(tok_bf.at[0, at], tok_bf.at[1, at], tok_send.at[n], tok_recv.at[n], (mate, col))

    for n in range(pieces):
        lax.fori_loop(n * (height // group // pieces), (n + 1) * (height // group // pieces), close_rows, 0)
        tok_copy(n).start()
    tok_out_copy = local(tok_map, tok_out, 7)
    tok_out_copy.start()

    kv_width = w_kv.shape[-1]

    def project(block, side):
        out = jnp.dot(
            tok_bf[side], wide(g_kv, block // 2, 0, kv_width), preferred_element_type=jnp.float32
        )
        kv[block // 2, pl.ds(side * count, count), :] = out.astype(jnp.bfloat16)

    @pl.when(col % 2 == core)
    def _():
        kv_copy.wait()

    finish(ff_jobs)
    finish(ff_jobs + 1)
    project(near, 0)
    for n in range(pieces):
        tok_copy(n).wait_recv()
    project(near, 1)
    finish(ff_jobs + 2)
    finish(ff_jobs + 3)
    for side in range(2):
        project(far, side)
    queries_copy.wait()

    latents = queries.shape[0]
    scale = 1.0 / math.sqrt(HEAD)
    lane = lax.broadcasted_iota(jnp.int32, (1, LANES), 1)
    pairs = half // LANES
    stat_lanes = pl.ds(half, LANES)
    step_rows = latents // 2
    share = latents // (rows // 2 * cols)

    def attend(pair):
        lanes = pl.ds(pair * LANES, LANES)

        def one(n, carry):
            at = pl.ds(pl.multiple_of(n * step_rows, 16), step_rows)
            q = queries[at, lanes]
            keys = kv[0, :, lanes]
            vals = kv[1, :, lanes]
            base = jnp.zeros((step_rows, LANES), jnp.float32) if pair == 0 else stat[at, :]
            outs = []
            for s in range(2):
                keep = (lane // HEAD) == s
                q_one = jnp.where(keep, q, jnp.zeros_like(q))
                scores = lax.dot_general(
                    q_one, keys, (((1,), (1,)), ((), ())), preferred_element_type=jnp.float32
                )
                top = jnp.max(scores, axis=-1, keepdims=True)
                weights = jnp.exp2((scores - top) * (scale * LOG2E))
                den = jnp.sum(weights, axis=-1, keepdims=True)
                outs.append(
                    jnp.dot(weights.astype(jnp.bfloat16), vals, preferred_element_type=jnp.float32)
                )
                base = jnp.where(lane == pair * 2 + s, top * scale, base)
                base = jnp.where(lane == pair * 2 + s + 8, den, base)
            num[at, lanes] = jnp.where(lane < HEAD, outs[0], outs[1]).astype(jnp.bfloat16)
            if pair < pairs - 1:
                stat[at, :] = base
            else:
                high = base.astype(jnp.bfloat16).astype(jnp.float32)
                rest = base - high
                mid = rest.astype(jnp.bfloat16).astype(jnp.float32)
                low = rest - mid
                out = high + pltpu.roll(mid, 16, 1) + pltpu.roll(low, 32, 1)
                num[at, stat_lanes] = out.astype(jnp.bfloat16)
            return carry

        lax.fori_loop(0, latents // step_rows, one, 0)

    peers = [(i, j) for i in range(rows // 2) for j in range(cols) if i or j]

    def sum_copy(i, j, part):
        to_chip, to_col = (chip + i) % (rows // 2), (col + j) % cols
        slot = i * cols + j
        give = pl.ds(pl.multiple_of((to_chip * cols + to_col) * share, 16), share)
        size = LANES if part < pairs - 1 else 2 * LANES
        lanes = pl.ds(part * LANES, size)
        at = slot * pairs + part
        return remote(
            num.at[give, lanes],
            got.at[slot, :, lanes],
            sum_send.at[at],
            sum_recv.at[at],
            (to_chip * 2 + core, to_col),
        )

    for pair in range(pairs):
        attend(pair)
        for i, j in peers:
            sum_copy(i, j, pair).start()
        if pair == 0:
            until("b", len(jobs) - 1)
    while plan:
        run()

    for i, (dr, dc, cond) in enumerate(halo):

        @pl.when(cond)
        def _():
            halo_copy(i, dr, dc).wait_send()

    z_wait()

    def sent(j):
        for leg in range(4 if j < ff_jobs else 3):
            if leg != 2 or not is_wide(j):
                hop(j, leg).wait_send()
        cond, nxt = onward(j)

        @pl.when(cond)
        def _():
            for across in (False, True) if is_wide(j) else (False,):
                z_pass(j, nxt, across).wait_send()

    for j in range(len(jobs)):
        given(j, functools.partial(sent, j))
    for n in range(pieces):
        tok_copy(n).wait_send()
    tok_out_copy.wait()

    @pl.when(col // 2 == core)
    def _():
        o_copy.wait()

    def own_rows(at_chip, at_col):
        return pl.ds(pl.multiple_of((at_chip * cols + at_col) * share, 16), share)

    def spread(factor):
        parts = []
        for pair in range(pairs):
            lo = jnp.broadcast_to(factor[:, 2 * pair : 2 * pair + 1], (share, LANES))
            hi = jnp.broadcast_to(factor[:, 2 * pair + 1 : 2 * pair + 2], (share, LANES))
            parts.append(jnp.where(lane < HEAD, lo, hi))
        return jnp.concatenate(parts, axis=-1)

    for i, j in peers:
        for part in range(pairs):
            sum_copy(i, j, part).wait_recv()
    mine = own_rows(chip, col)
    slots = [None] + [i * cols + j for i, j in peers]

    def source(slot, lanes):
        value = num[mine, lanes] if slot is None else got[slot, :, lanes]
        return value.astype(jnp.float32)

    stats = []
    for slot in slots:
        s = source(slot, stat_lanes)
        stats.append(s + (pltpu.roll(s, LANES - 16, 1) + pltpu.roll(s, LANES - 32, 1)))
    peak = functools.reduce(jnp.maximum, stats)
    den, total = None, None
    for slot, s in zip(slots, stats):
        factor = jnp.exp(s - peak)
        d = pltpu.roll(s, LANES - 8, 1) * factor
        t = source(slot, pl.ds(0, half)) * spread(factor)
        den = d if den is None else den + d
        total = t if total is None else total + t
    att[core] = total / spread(den)
    n_sum = len(slots) * pairs
    swap = remote(att.at[core], att.at[core], sum_send.at[n_sum], sum_recv.at[n_sum], (mate, col))
    swap.start()
    for i, j in peers:
        for part in range(pairs):
            sum_copy(i, j, part).wait_send()
    remote(
        att.at[1 - core], att.at[1 - core], sum_send.at[n_sum], sum_recv.at[n_sum], (mate, col)
    ).wait_recv()
    first, second = att[0], att[1]
    squares = (
        jnp.sum(first * first, axis=-1, keepdims=True)
        + jnp.sum(second * second, axis=-1, keepdims=True)
    ) / depth
    inverse = lax.rsqrt(squares + 1e-06)
    scaled = jnp.concatenate([first, second], axis=-1) * inverse * latent_gain[...][None, :]
    turned = g_o[...].reshape(half, depth)
    done = lax.dot_general(
        scaled.astype(jnp.bfloat16), turned, (((1,), (1,)), ((), ())), preferred_element_type=jnp.float32
    )
    lat[mine, core_lanes] = done.astype(jnp.bfloat16)

    planes = [col] + blocks
    chips = [chip, x_row // 2, y_row // 2, d_row // 2]
    ways = [x_row, y_row, d_row]

    def out_copy_z(k):
        ref = lat.at[mine, core_lanes]
        return remote(ref, ref, out_send.at[k], out_recv.at[col], (row, blocks[k]))

    base_p, base_c = cols, cols + 3 * cols

    def out_copy_plane(n, way):
        ref = lat.at[own_rows(chip, planes[n]), core_lanes]
        at = base_p + n * 3 + way
        return remote(ref, ref, out_send.at[at], out_recv.at[at], (ways[way], col))

    def out_landed_plane(n, way):
        ref = lat.at[own_rows(chips[way + 1], planes[n]), core_lanes]
        at = base_p + n * 3 + way
        return remote(ref, ref, out_send.at[at], out_recv.at[at], (mate, col))

    mate_lanes = pl.ds(pl.multiple_of((1 - core) * half, LANES), half)

    def out_copy_core(n, who, lanes):
        ref = lat.at[own_rows(chips[who], planes[n]), lanes]
        at = base_c + n * 4 + who
        return remote(ref, ref, out_send.at[at], out_recv.at[at], (mate, col))

    def fan(n):
        for way in range(3):
            out_copy_plane(n, way).start()
        out_copy_core(n, 0, core_lanes).start()

    for k in range(cols - 1):
        out_copy_z(k).start()
    fan(0)
    for k in range(cols - 1):
        ref = lat.at[own_rows(chip, blocks[k]), core_lanes]
        remote(ref, ref, out_send.at[0], out_recv.at[blocks[k]], (mate, col)).wait_recv()
        fan(k + 1)
    for n in range(cols):
        for way in range(3):
            out_landed_plane(n, way).wait_recv()
            out_copy_core(n, way + 1, core_lanes).start()
    swap.wait_send()
    for k in range(cols - 1):
        out_copy_z(k).wait_send()
    for n in range(cols):
        for way in range(3):
            out_copy_plane(n, way).wait_send()
    for n in range(cols):
        for who in range(4):
            out_copy_core(n, who, mate_lanes).wait_recv()
            out_copy_core(n, who, core_lanes).wait_send()


def hand_over(tok_in, lat_in, tok, lat, tok_v, lat_v, sem):
    pieces = []
    for src, mid, dst in ((tok_in, tok_v, tok), (lat_in, lat_v, lat)):
        n = src.shape[0] // 2
        for i in range(2):
            at = pl.ds(i * n, n)
            k = 2 * len(pieces)
            pieces.append(
                (
                    pltpu.make_async_copy(src.at[at], mid.at[at], sem.at[k]),
                    pltpu.make_async_copy(mid.at[at], dst.at[at], sem.at[k + 1]),
                )
            )
    for c, _ in pieces:
        c.start()
    for c, d in pieces:
        c.wait()
        d.start()
    for _, d in pieces:
        d.wait()


def hbm(n):
    return [pl.BlockSpec(memory_space=pl.ANY)] * n


def vmem(n):
    return [pl.BlockSpec(memory_space=pltpu.VMEM)] * n


def fits(mesh_rows, mesh_cols, tokens, w_in, w_out, w_kv, queries, w_o):
    height, width, depth = tokens.shape
    return (
        mesh_rows == 8
        and mesh_cols == 4
        and depth == HEADS * HEAD
        and depth % 256 == 0
        and depth % (2 * LANES) == 0
        and w_in.shape[1] % LANES == 0
        and w_out.shape[0] % (32 * mesh_rows) == 0
        and depth % (32 * mesh_rows) == 0
        and w_kv.shape[1] * 2 == depth
        and w_o.shape[1] % 64 == 0
        and w_o.shape[1] * mesh_cols == depth
        and queries.shape[0] % (16 * mesh_rows // 2 * mesh_cols) == 0
        and height % 16 == 0
        and width % 8 == 0
        and height * width % 32 == 0
    )


def kernel_body(tokens, dw_kernel, norm_gain, norm_shift, w_in, w_out, w_kv, queries, latent_gain, w_o):
    rows, cols = lax.axis_size("row"), lax.axis_size("col")
    height, width, depth = tokens.shape
    if not fits(rows, cols, tokens, w_in, w_out, w_kv, queries, w_o):
        return body(
            tokens, dw_kernel, norm_gain, norm_shift, w_in, w_out, w_kv, queries, latent_gain, w_o
        )
    count = height * width
    latents = queries.shape[0]
    f_width = w_in.shape[1]
    half = depth // 2
    bf16, f32 = jnp.bfloat16, jnp.float32

    def cut(w, lead):
        size = w.shape[0]
        for n in lead:
            size //= n
        return w.reshape(lead + (size, w.shape[1]))

    shards = [
        cut(w_in, (2, 2, 2, 2)),
        cut(w_out, (2, 2, 2, 2)),
        cut(w_kv, (2, 2, 2)),
        cut(w_o.T, (2, 2)),
    ]
    share = latents // (rows // 2 * cols)
    pairs = half // LANES
    n_jobs = 4 * (cols - 1) + 4 + 2
    n_sum = rows // 2 * cols * pairs + 1
    n_out = cols + 3 * cols + 4 * cols
    dma = pltpu.SemaphoreType.DMA
    outs = pl.pallas_call(
        functools.partial(block_kernel, rows, cols),
        out_shape=(
            jax.ShapeDtypeStruct(tokens.shape, bf16),
            jax.ShapeDtypeStruct((latents, depth), bf16),
        ),
        in_specs=hbm(2) + vmem(2) + hbm(5) + vmem(1),
        out_specs=(hbm(1)[0], vmem(1)[0]),
        scratch_shapes=[
            pltpu.VMEM(tokens.shape, bf16),
            pltpu.VMEM(dw_kernel.shape, f32),
            pltpu.VMEM((latents, half), bf16),
            pltpu.VMEM((cols,) + shards[0].shape, bf16),
            pltpu.VMEM((cols,) + shards[1].shape, bf16),
            pltpu.VMEM((2,) + shards[2].shape, bf16),
            pltpu.VMEM((2,) + shards[3].shape, bf16),
            pltpu.VMEM((height + 2 * HALO, width + 2 * EDGE, depth), f32),
            pltpu.VMEM((height, width, depth), f32),
            pltpu.VMEM((count, depth), bf16),
            pltpu.VMEM((count, f_width), bf16),
            pltpu.VMEM((count, depth), f32),
            pltpu.VMEM((height, width, depth), bf16),
            pltpu.VMEM((2, count, depth), bf16),
            pltpu.VMEM((2, 2 * count, half), bf16),
            pltpu.VMEM((2, HALO, width, depth), bf16),
            pltpu.VMEM((2, HALO, height, depth), bf16),
            pltpu.VMEM((2, HALO, height, depth), bf16),
            pltpu.VMEM((4, HALO, EDGE, depth), bf16),
            pltpu.VMEM((latents, half + LANES), bf16),
            pltpu.VMEM((latents, LANES), f32),
            pltpu.VMEM((rows // 2 * cols, share, half + LANES), bf16),
            pltpu.VMEM((2, share, half), f32),
            dma((8,)),
            dma((8,)),
            dma((2 * (14 + n_jobs),)),
            dma((2 * (4 * cols + 6),)),
            dma((n_jobs * 4,)),
            dma((n_jobs * 4,)),
            dma((2,)),
            dma((2,)),
            dma((n_sum,)),
            dma((n_sum,)),
            dma((n_out,)),
            dma((n_out,)),
            dma((8,)),
        ],
        compiler_params=pltpu.CompilerParams(
            collective_id=0, has_side_effects=True, vmem_limit_bytes=VMEM_BYTES
        ),
        name="block",
    )(
        tokens,
        dw_kernel,
        norm_gain,
        norm_shift,
        *shards,
        queries,
        latent_gain,
    )
    return tuple(
        pl.pallas_call(
            hand_over,
            out_shape=tuple(jax.ShapeDtypeStruct(o.shape, o.dtype) for o in outs),
            in_specs=hbm(2),
            out_specs=tuple(hbm(2)),
            scratch_shapes=[pltpu.VMEM(o.shape, o.dtype) for o in outs] + [dma((8,))],
            name="hand_over",
        )(*outs)
    )


def with_halo(cells, sides, width):
    for axis, dim in sides:
        count = lax.axis_size(axis)
        ends = count - 1
        head = lax.slice_in_dim(cells, 0, width, axis=dim)
        tail = lax.slice_in_dim(cells, cells.shape[dim] - width, cells.shape[dim], axis=dim)
        cells = jnp.concatenate(
            [
                lax.ppermute(tail, axis, [(i, (i + 1) % count) for i in range(ends)]),
                cells,
                lax.ppermute(head, axis, [((i + 1) % count, i) for i in range(ends)]),
            ],
            axis=dim,
        )
    return cells


def conv_taps(padded, height, width, dw_kernel):
    mixed = jnp.zeros((height, width, padded.shape[2]), jnp.float32)
    for row_tap in range(7):
        for col_tap in range(7):
            mixed = (
                mixed
                + padded[row_tap : row_tap + height, col_tap : col_tap + width]
                * dw_kernel[row_tap, col_tap]
            )
    return mixed


def layer_norm(mixed, norm_gain, norm_shift):
    center = mixed - jnp.mean(mixed, axis=-1, keepdims=True)
    spread = jnp.mean(center * center, axis=-1, keepdims=True)
    return (center * lax.rsqrt(spread + 1e-06) * norm_gain + norm_shift).astype(jnp.bfloat16)


def finish_latents(numer, denom, latent_gain, w_full):
    attended = (numer / denom[..., None]).reshape(numer.shape[0], -1)
    squares = jnp.mean(attended * attended, axis=-1, keepdims=True)
    scaled = (attended * lax.rsqrt(squares + 1e-06) * latent_gain).astype(jnp.bfloat16)
    return jnp.dot(scaled, w_full, preferred_element_type=jnp.float32).astype(jnp.bfloat16)


def body(tokens, dw_kernel, norm_gain, norm_shift, w_in, w_out, w_kv, queries, latent_gain, w_o):
    height, width, width_d = tokens.shape
    latent_count = queries.shape[0]
    padded = with_halo(tokens, (("row", 0), ("col", 1)), 3)
    mixed = conv_taps(padded.astype(jnp.float32), height, width, dw_kernel)
    normed = layer_norm(mixed, norm_gain, norm_shift).reshape(height * width, width_d)
    residual = tokens.reshape(height * width, width_d).astype(jnp.float32)
    hidden = jax.nn.gelu(
        jnp.dot(
            normed,
            lax.all_gather(w_in, "col", axis=1, tiled=True),
            preferred_element_type=jnp.float32,
        )
    ).astype(jnp.bfloat16)
    update = jnp.dot(
        hidden, lax.all_gather(w_out, "col", axis=0, tiled=True), preferred_element_type=jnp.float32
    )
    token_rows = (residual + update).astype(jnp.bfloat16)
    token_map = token_rows.reshape(height, width, width_d)
    keys_vals = jnp.dot(
        token_rows,
        lax.all_gather(w_kv, "col", axis=1, tiled=True),
        preferred_element_type=jnp.float32,
    ).astype(jnp.bfloat16)
    w_full = lax.all_gather(w_o, "col", axis=1, tiled=True)
    key_heads = keys_vals[:, :width_d].reshape(-1, HEADS, HEAD)
    val_heads = keys_vals[:, width_d:].reshape(-1, HEADS, HEAD)
    query_heads = queries.reshape(latent_count, HEADS, HEAD)
    score_scale = 1.0 / math.sqrt(HEAD)
    group_size = math.gcd(HEADS, 4)
    max_parts, den_parts, num_parts = ([], [], [])
    for first_head in range(0, HEADS, group_size):
        scores = (
            jnp.einsum(
                "lhd,thd->lht",
                query_heads[:, first_head : first_head + group_size],
                key_heads[:, first_head : first_head + group_size],
                preferred_element_type=jnp.float32,
            )
            * score_scale
        )
        local_max = jnp.max(scores, axis=-1)
        weights = jnp.exp(scores - local_max[..., None])
        den_parts.append(jnp.sum(weights, axis=-1))
        max_parts.append(local_max)
        num_parts.append(
            jnp.einsum(
                "lht,thd->lhd",
                weights.astype(jnp.bfloat16),
                val_heads[:, first_head : first_head + group_size],
                preferred_element_type=jnp.float32,
            )
        )
    maxima = jnp.concatenate(max_parts, axis=1)
    denom = jnp.concatenate(den_parts, axis=1)
    numer = jnp.concatenate(num_parts, axis=1)
    peak = lax.pmax(maxima, ("row", "col"))
    factor = jnp.exp(maxima - peak)
    den_terms = denom * factor
    num_terms = (numer * factor[..., None]).reshape(latent_count, width_d)
    den_part, num_part = (
        lax.psum_scatter(den_terms, "col", scatter_dimension=0, tiled=True),
        lax.psum_scatter(num_terms, "col", scatter_dimension=0, tiled=True),
    )
    den_share, num_share = lax.psum((den_part, num_part), "row")
    own_rows = finish_latents(
        num_share.reshape(num_share.shape[0], HEADS, HEAD), den_share, latent_gain, w_full
    )
    latents = lax.all_gather(own_rows, "col", axis=0, tiled=True)
    return (token_map, latents)


def solution(mesh):
    in_specs = (
        P("row", "col", None),
        P(),
        P(),
        P(),
        P(None, "col"),
        P("col", None),
        P(None, "col"),
        P(),
        P(),
        P(None, "col"),
    )
    out_specs = (P("row", "col", None), P())
    return jax.shard_map(kernel_body, mesh=mesh, in_specs=in_specs, out_specs=out_specs, check_vma=False)
```

```python
import functools
import math

import jax
import jax.numpy as jnp
from jax import lax
from jax.experimental import pallas as pl
from jax.experimental.pallas import tpu as pltpu
from jax.sharding import PartitionSpec as P

HEADS = 12
HEAD = 64
HALO = 3
LOG2E = math.log2(math.e)
EDGE = 8
LANES = 128
MESH = pl.DeviceIdType.MESH
VMEM_BYTES = 60 * 1024 * 1024


CONV_PARTS = 4
WIDE = (3, 4, 5)
HALO_AFTER = 4
PRE = 3
Z_LAST = 19
LAG_B = 2
LAG_C = 4


def block_kernel(
    rows,
    cols,
    tokens_in,
    dw_in,
    gain,
    shift,
    w_in,
    w_out,
    w_kv,
    w_o,
    queries_in,
    latent_gain,
    tok_out,
    lat,
    tokens,
    dw,
    queries,
    g_in,
    g_out,
    g_kv,
    g_o,
    pad,
    mixed,
    normed,
    hidden,
    acc,
    tok_map,
    tok_bf,
    kv,
    h_rows,
    h_cols,
    col_out,
    h_corners,
    num,
    stat,
    got,
    stat_out,
    got_stat,
    att,
    halo_send,
    halo_recv,
    z_send,
    z_recv,
    hop_send,
    hop_recv,
    tok_send,
    tok_recv,
    sum_send,
    sum_recv,
    out_send,
    out_recv,
    local_sem,
):
    row, col = lax.axis_index("row"), lax.axis_index("col")
    height, width, depth = tokens.shape
    count = height * width
    y, x, core = row // 4, (row // 2) % 2, row % 2
    chip = row // 2
    half = depth // 2
    x_row = row + 2 * (1 - 2 * x)
    y_row = row + 4 * (1 - 2 * y)
    d_row = row + 2 * (1 - 2 * x) + 4 * (1 - 2 * y)
    mate = row + 1 - 2 * core

    def remote(src, dst, send, recv, device):
        return pltpu.make_async_remote_copy(
            src_ref=src,
            dst_ref=dst,
            send_sem=send,
            recv_sem=recv,
            device_id=device,
            device_id_type=MESH,
        )

    def local(src, dst, i):
        return pltpu.make_async_copy(src, dst, local_sem.at[i])

    core_lanes = pl.ds(pl.multiple_of(core * half, LANES), half)
    tokens_copy = local(tokens_in, tokens, 0)
    dw_copy = local(dw_in, dw, 1)
    queries_copy = local(queries_in.at[:, core_lanes], queries, 2)
    in_copy = local(w_in, g_in.at[col], 3)
    out_copy = local(w_out, g_out.at[col], 4)
    kv_copy = local(w_kv, g_kv.at[col // 2], 5)
    o_copy = local(w_o, g_o.at[col % 2], 6)
    for copy in (tokens_copy, dw_copy, queries_copy, in_copy, out_copy):
        copy.start()

    @pl.when(col % 2 == core)
    def _():
        kv_copy.start()

    @pl.when(col // 2 == core)
    def _():
        o_copy.start()

    both = jnp.minimum(col, cols - 1 - col)
    longer = jnp.where(cols - 1 - col > col, 1, -1)
    blocks = []
    for k in range(cols - 1):
        paired = k < 2 * both
        side = jnp.where(paired, 1 - 2 * (k % 2), longer)
        gap = jnp.where(paired, k // 2 + 1, k - both + 1)
        blocks.append(col + side * gap)

    halo = []
    for dr in (-1, 0, 1):
        for dc in (-1, 0, 1):
            if dr == 0 and dc == 0:
                continue
            cond = None
            for d, pos, n in ((dr, row, rows), (dc, col, cols)):
                if d:
                    one = (pos + d >= 0) & (pos + d < n)
                    cond = one if cond is None else cond & one
            halo.append((dr, dc, cond))

    barrier = pltpu.get_barrier_semaphore()
    peers = [(None, (x_row, col)), (None, (y_row, col)), (None, (mate, col))]
    for dr, dc, cond in halo:
        if dc == 0:
            cond = cond & (row + dr != mate) & (row + dr != x_row) & (row + dr != y_row)
        peers.append((cond, (row + dr, col + dc)))
    greeted = 0
    for cond, device in peers:
        if cond is None:
            pl.semaphore_signal(barrier, inc=1, device_id=device, device_id_type=MESH)
            greeted = greeted + 1
        else:

            @pl.when(cond)
            def _():
                pl.semaphore_signal(barrier, inc=1, device_id=device, device_id_type=MESH)

            greeted = greeted + jnp.where(cond, 1, 0)

    def halo_slot(dr, dc):
        if dc == 0:
            return h_rows.at[0 if dr < 0 else 1]
        if dr == 0:
            return h_cols.at[0 if dc < 0 else 1]
        return h_corners.at[(0 if dr < 0 else 2) + (0 if dc < 0 else 1)]

    def halo_copy(i, dr, dc):
        r_span = {-1: pl.ds(0, HALO), 0: slice(None), 1: pl.ds(height - HALO, HALO)}[dr]
        c_span = {-1: pl.ds(0, EDGE), 0: slice(None), 1: pl.ds(width - EDGE, EDGE)}[dc]
        return remote(
            tokens.at[r_span, c_span] if dr or not dc else col_out.at[0 if dc < 0 else 1],
            halo_slot(-dr, -dc),
            halo_send.at[i],
            halo_recv.at[len(halo) - 1 - i],
            (row + dr, col + dc),
        )

    def own_unit(part, across=False):
        yy, xx = (1 - y, 1 - x) if across else (y, x)
        if part < 4:
            w = (w_in, w_out)[part // 2]
            return w.at[yy, xx, core, part % 2], (g_in, g_out)[part // 2].at[col, yy, xx, core, part % 2]
        if part < 6:
            return w_kv.at[yy, xx, part - 4], g_kv.at[col // 2, yy, xx, part - 4]
        return w_o.at[yy, xx], g_o.at[col % 2, yy, xx]

    def z_id(block, part):
        if part < 4:
            return block * 4 + part
        if part < 6:
            return 4 * cols + (block // 2) * 2 + part - 4
        return 4 * cols + 4 + block % 2

    ff_jobs = 4 * (cols - 1)
    n_send, n_recv = 14 + ff_jobs + 6, 4 * cols + 6

    def z_copies(part, side):
        made = []
        for across in (False, True) if part in WIDE else (False,):
            src, dst = own_unit(part, across)
            at = part * 2 + (0 if side > 0 else 1) + (n_send if across else 0)
            into = z_id(col, part) + (n_recv if across else 0)
            made.append(remote(src, dst, z_send.at[at], z_recv.at[into], (row, col + side)))
        return made

    def z_given(part, side, act):
        cond = (col + side >= 0) & (col + side < cols)
        if part >= 4:
            cond = cond & ((col % 2 if part < 6 else col // 2) == core)

        @pl.when(cond)
        def _():
            for c in z_copies(part, side):
                act(c)

    def z_start(part):
        for side in (-1, 1):
            z_given(part, side, lambda c: c.start())

    def z_wait():
        for part in range(7):
            for side in (-1, 1):
                z_given(part, side, lambda c: c.wait_send())

    near = jnp.where(col < cols // 2, core, core + 2)
    far = jnp.where(col < cols // 2, core + 2, core)
    jobs = [(blocks[k], p) for k in range(cols - 1) for p in range(4)]
    jobs += [(near, 4), (near, 5), (far, 4), (far, 5)]
    jobs += [(core * 2, 6), (core * 2 + 1, 6)]

    def unit(j, dy, dx):
        block, part = jobs[j]
        yy, xx = (1 - y if dy else y), (1 - x if dx else x)
        if part < 4:
            return (g_in, g_out)[part // 2].at[block, yy, xx, core, part % 2]
        if part < 6:
            return g_kv.at[block // 2, yy, xx, part - 4]
        return g_o.at[block % 2, yy, xx]

    def turn(j):
        part = jobs[j][1]
        return j % 2 if part == 6 or 3 in WIDE else part % 2

    def hop(j, leg):
        at = j * 4 + leg
        if leg == 3:
            block, part = jobs[j]
            ref = (g_in, g_out)[part // 2].at[block, :, :, core, part % 2]
            device = mate
        elif leg == 2:
            ref = unit(j, 0, 1) if turn(j) == 0 else unit(j, 1, 0)
            device = y_row if turn(j) == 0 else x_row
        else:
            ref = unit(j, 0, 0)
            device = x_row if leg == 0 else y_row
        return remote(ref, ref, hop_send.at[at], hop_recv.at[at], (device, col))

    def landed(j, leg):
        at = j * 4 + leg
        if leg == 3:
            block, part = jobs[j]
            ref = (g_in, g_out)[part // 2].at[block, :, :, 1 - core, part % 2]
        elif leg == 2:
            ref = unit(j, 1, 1)
        else:
            ref = unit(j, 0, 1) if leg == 0 else unit(j, 1, 0)
        return remote(ref, ref, hop_send.at[at], hop_recv.at[at], (mate, col))

    def onward(j):
        block = jobs[j][0]
        nxt = col + jnp.where(col > block, 1, -1)
        return (block != col) & (nxt >= 0) & (nxt < cols), nxt

    def is_wide(j):
        return jobs[j][1] in WIDE

    def z_arrival(j, across=False):
        block, part = jobs[j]
        ref = unit(j, 1, 1) if across else unit(j, 0, 0)
        at = z_id(block, part) + (n_recv if across else 0)
        return remote(ref, ref, z_send.at[0], z_recv.at[at], (mate, col))

    def z_pass(j, nxt, across=False):
        block, part = jobs[j]
        ref = unit(j, 1, 1) if across else unit(j, 0, 0)
        at = z_id(block, part) + (n_recv if across else 0)
        by = 14 + j + (n_send if across else 0)
        return remote(ref, ref, z_send.at[by], z_recv.at[at], (row, nxt))

    def step_z(j, gap=None):
        cond, nxt = onward(j)
        if gap is not None:
            block = jobs[j][0]
            cond = cond & (jnp.where(col > block, col - block, block - col) == gap)

        @pl.when(cond)
        def _():
            for across in (False, True) if is_wide(j) else (False,):
                z_arrival(j, across).wait_recv()
                z_pass(j, nxt, across).start()

    def given(j, act):
        if j < ff_jobs:
            act()
        else:
            pl.when(jobs[j][0] != col)(act)

    def step_a(j):
        @pl.when(jnp.logical_not(onward(j)[0]))
        def _():
            z_arrival(j).wait_recv()

        hop(j, 0).start()
        hop(j, 1).start()

    def step_b(j):
        if not is_wide(j):
            landed(j, turn(j)).wait_recv()
            hop(j, 2).start()

    def step_c(j):
        if is_wide(j):
            landed(j, 0).wait_recv()
            landed(j, 1).wait_recv()

            @pl.when(jnp.logical_not(onward(j)[0]))
            def _():
                z_arrival(j, True).wait_recv()

        else:
            landed(j, 1 - turn(j)).wait_recv()
            landed(j, 2).wait_recv()
        if j < ff_jobs:
            hop(j, 3).start()

    last = ff_jobs + 4
    z_starts = {p: p - 2 for p in range(max(HALO_AFTER, 2), 4)} | {4: 4, 5: 5, 6: 9}
    passes = [(4 * r + p, p + (0, 1, 3)[r], None) for r in range(cols - 1) for p in range(4)]
    passes += [(ff_jobs, 8, None), (ff_jobs + 1, 9, None), (ff_jobs + 2, 10, None), (ff_jobs + 3, 11, None)]
    passes += [(last + i, 14 + 3 * d, d + 1) for i in range(2) for d in range(2)]

    def z_tick(t):
        for part, at in z_starts.items():
            if at == t:
                z_start(part)
        for j, at, gap in passes:
            if at == t:
                step_z(j, gap)

    steps = {"z": z_tick, "a": step_a, "b": step_b, "c": step_c}
    plan = []
    for t in range(last):
        plan.append(("z", t))
        for name, lag in (("a", 0), ("b", LAG_B), ("c", LAG_C)):
            if t - lag >= 0:
                plan.append((name, t - lag))
        plan.append(("tick", t))
    for t in range(last, last + LAG_B):
        plan.append(("z", t))
        plan.append(("b", t - LAG_B))
        if t - LAG_C >= 0:
            plan.append(("c", t - LAG_C))
    for t in range(last + LAG_B, Z_LAST):
        plan.append(("z", t))
    plan += [("a", j) for j in range(last, len(jobs))]
    plan += [("c", j) for j in range(last + LAG_B - LAG_C, last)]
    plan += [("b", j) for j in range(last, len(jobs))]
    plan += [("c", j) for j in range(last, len(jobs))]

    def run():
        name, j = plan.pop(0)
        if name == "z":
            z_tick(j)
        elif name != "tick":
            given(j, functools.partial(steps[name], j))
        return name, j

    def tick():
        while plan and run()[0] != "tick":
            pass

    def until(name, j):
        while (name, j) in plan:
            run()

    def finish(j):
        until("c", j)
        if j < ff_jobs:
            landed(j, 3).wait_recv()

    tokens_copy.wait()
    pad[pl.ds(HALO, height), pl.ds(EDGE, width), :] = tokens[...].astype(jnp.float32)
    for side in range(2):
        edge = pl.ds(side * (EDGE + width), EDGE)
        pad[pl.ds(HALO, height), edge, :] = jnp.zeros((height, EDGE, depth), jnp.float32)
        for n in range(HALO):
            at = EDGE + (n if side == 0 else width - HALO + n)
            col_out[side, n] = pad[pl.ds(HALO, height), at, :].astype(jnp.bfloat16)
    pl.semaphore_wait(barrier, greeted)

    for part in range(HALO_AFTER):
        z_start(part)
    for i, (dr, dc, cond) in enumerate(halo):

        @pl.when(cond)
        def _():
            halo_copy(i, dr, dc).start()

    for part in range(HALO_AFTER, 2):
        z_start(part)
    for _ in range(PRE):
        tick()

    spans = {-1: (0, HALO), 0: (HALO, height), 1: (HALO + height, HALO)}
    lanes_of = {-1: (0, EDGE), 0: (EDGE, width), 1: (EDGE + width, EDGE)}
    for i, (dr, dc, cond) in enumerate(halo):
        r0, rn = spans[dr]
        c0, cn = lanes_of[dc]

        @pl.when(cond)
        def _():
            halo_copy(len(halo) - 1 - i, -dr, -dc).wait_recv()
            if dr == 0:
                for n in range(HALO):
                    at = EDGE - HALO + n if dc < 0 else EDGE + width + n
                    side = 0 if dc < 0 else 1
                    pad[pl.ds(HALO, height), at, :] = h_cols[side, n].astype(jnp.float32)
            else:
                pad[pl.ds(r0, rn), pl.ds(c0, cn), :] = halo_slot(dr, dc)[...].astype(jnp.float32)

        if dr:

            @pl.when(jnp.logical_not(cond))
            def _():
                pad[pl.ds(r0, rn), pl.ds(c0, cn), :] = jnp.zeros((rn, cn, depth), jnp.float32)

    taps = 2 * HALO + 1
    chunks = depth // LANES
    dw_copy.wait()

    def conv_rows(first, n_rows):
        def one(step, carry):
            i = first + step // chunks
            q = pl.multiple_of((step % chunks) * LANES, LANES)
            sums = [None] * taps
            for a in range(taps):
                line = pad[i + a, :, pl.ds(q, LANES)]
                for b in range(taps):
                    lo = 0 if b < HALO else EDGE
                    hi = EDGE + width + (EDGE if b > HALO else 0)
                    term = line[lo:hi] * dw[a, pl.ds(b, 1), pl.ds(q, LANES)]
                    sums[b] = term if sums[b] is None else sums[b] + term
            total = sums[HALO]
            for b in range(taps):
                if b == HALO:
                    continue
                size = width + EDGE
                offset = EDGE - HALO + b - (0 if b < HALO else EDGE)
                total = total + pltpu.roll(sums[b], (size - offset) % size, 0)[:width]
            mixed[i, :, pl.ds(q, LANES)] = total
            return carry

        lax.fori_loop(0, n_rows * chunks, one, 0, unroll=2)

    group = 2
    span = group * width

    def norm_rows(g, carry):
        value = mixed[pl.ds(g * group, group), :, :].reshape(span, depth)
        center = value - jnp.mean(value, axis=-1, keepdims=True)
        spread = jnp.mean(center * center, axis=-1, keepdims=True)
        out = center * lax.rsqrt(spread + 1e-06) * gain[...][None, :] + shift[...][None, :]
        normed[pl.ds(pl.multiple_of(g * span, 16), span), :] = out.astype(jnp.bfloat16)
        return carry

    tick()
    parts = CONV_PARTS
    for part in range(parts):
        conv_rows(part * (height // parts), height // parts)
        tick()
    half_groups = height // group // 2
    lax.fori_loop(0, half_groups, norm_rows, 0)
    tick()
    lax.fori_loop(half_groups, 2 * half_groups, norm_rows, 0)
    tick()
    in_copy.wait()
    out_copy.wait()

    def wide(ref, block, lo, size):
        value = ref[(block,) + (slice(None),) * (len(ref.shape) - 2) + (pl.ds(lo, size),)]
        return value.reshape(-1, size)

    f_width = w_in.shape[-1]
    tile = 256 if f_width % 256 == 0 else LANES

    def expand(block):
        def one(n, carry):
            lo = pl.multiple_of(n * tile, tile)
            u = jnp.dot(normed[...], wide(g_in, block, lo, tile), preferred_element_type=jnp.float32)
            hidden[:, pl.ds(lo, tile)] = jax.nn.gelu(u).astype(jnp.bfloat16)
            return carry

        lax.fori_loop(0, f_width // tile, one, 0, unroll=True)

    def contract(block, fresh):
        def one(n, carry):
            lo = pl.multiple_of(n * 256, 256)
            part = jnp.dot(
                hidden[...], wide(g_out, block, lo, 256), preferred_element_type=jnp.float32
            )
            if fresh:
                acc[:, pl.ds(lo, 256)] = part
            else:
                acc[:, pl.ds(lo, 256)] += part
            return carry

        lax.fori_loop(0, depth // 256, one, 0, unroll=True)

    expand(col)
    tick()
    contract(col, True)
    tick()
    for k in range(cols - 1):
        finish(4 * k)
        finish(4 * k + 1)
        expand(blocks[k])
        finish(4 * k + 2)
        finish(4 * k + 3)
        contract(blocks[k], False)

    def close_rows(g, carry):
        base = pad[pl.ds(HALO + g * group, group), pl.ds(EDGE, width), :].reshape(span, depth)
        at = pl.ds(pl.multiple_of(g * span, 16), span)
        total = base + acc[at, :]
        tok_map[pl.ds(g * group, group), :, :] = total.reshape(group, width, depth).astype(jnp.bfloat16)
        tok_bf[0, at, :] = total.astype(jnp.bfloat16)
        return carry

    pieces = 2
    piece = count // pieces

    def tok_copy(n):
        at = pl.ds(n * piece, piece)
        return remote(tok_bf.at[0, at], tok_bf.at[1, at], tok_send.at[n], tok_recv.at[n], (mate, col))

    for n in range(pieces):
        lax.fori_loop(n * (height // group // pieces), (n + 1) * (height // group // pieces), close_rows, 0)
        tok_copy(n).start()
    tok_out_copy = local(tok_map, tok_out, 7)
    tok_out_copy.start()

    kv_width = w_kv.shape[-1]

    def project(block, side):
        out = jnp.dot(
            tok_bf[side], wide(g_kv, block // 2, 0, kv_width), preferred_element_type=jnp.float32
        )
        kv[block // 2, pl.ds(side * count, count), :] = out.astype(jnp.bfloat16)

    @pl.when(col % 2 == core)
    def _():
        kv_copy.wait()

    finish(ff_jobs)
    finish(ff_jobs + 1)
    project(near, 0)
    for n in range(pieces):
        tok_copy(n).wait_recv()
    project(near, 1)
    finish(ff_jobs + 2)
    finish(ff_jobs + 3)
    for side in range(2):
        project(far, side)
    queries_copy.wait()

    latents = queries.shape[0]
    scale = 1.0 / math.sqrt(HEAD)
    lane = lax.broadcasted_iota(jnp.int32, (1, LANES), 1)
    pairs = half // LANES
    step_rows = latents // 2
    share = latents // (rows // 2 * cols)

    def attend(pair):
        lanes = pl.ds(pair * LANES, LANES)

        def one(n, carry):
            at = pl.ds(pl.multiple_of(n * step_rows, 16), step_rows)
            q = queries[at, lanes]
            keys = kv[0, :, lanes]
            vals = kv[1, :, lanes]
            base = jnp.zeros((step_rows, LANES), jnp.float32) if pair == 0 else stat[at, :]
            outs = []
            for s in range(2):
                keep = (lane // HEAD) == s
                q_one = jnp.where(keep, q, jnp.zeros_like(q))
                scores = lax.dot_general(
                    q_one, keys, (((1,), (1,)), ((), ())), preferred_element_type=jnp.float32
                )
                top = jnp.max(scores, axis=-1, keepdims=True)
                weights = jnp.exp2((scores - top) * (scale * LOG2E))
                vals_one = jnp.where(keep, vals, jnp.ones_like(vals))
                out = jnp.dot(
                    weights.astype(jnp.bfloat16), vals_one, preferred_element_type=jnp.float32
                )
                outs.append(out)
                base = jnp.where(lane == pair * 2 + s, top * scale, base)
                base = jnp.where(lane == pair * 2 + s + 8 + HEAD * (1 - s), out, base)
            num[at, lanes] = jnp.where(lane < HEAD, outs[0], outs[1]).astype(jnp.bfloat16)
            if pair < pairs - 1:
                stat[at, :] = base
            else:
                base = jnp.where(lane < 16, base + pltpu.roll(base, HEAD, 1), 0.0)
                high = base.astype(jnp.bfloat16).astype(jnp.float32)
                rest = base - high
                mid = rest.astype(jnp.bfloat16).astype(jnp.float32)
                low = rest - mid
                out = high + pltpu.roll(mid, 16, 1) + pltpu.roll(low, 32, 1)
                out = out.reshape(-1, share, LANES)
                packed = out[:, : share // 2] + pltpu.roll(out[:, share // 2 :], HEAD, 2)
                owners = step_rows // share
                stat_out[pl.ds(n * owners, owners)] = packed.astype(jnp.bfloat16)
            return carry

        lax.fori_loop(0, latents // step_rows, one, 0)

    peers = [(i, j) for i in range(rows // 2) for j in range(cols) if i or j]

    def sum_copy(i, j, part):
        to_chip, to_col = (chip + i) % (rows // 2), (col + j) % cols
        slot = i * cols + j
        give = pl.ds(pl.multiple_of((to_chip * cols + to_col) * share, 16), share)
        at = slot * (pairs + 1) + part
        if part == pairs:
            src, dst = stat_out.at[to_chip * cols + to_col], got_stat.at[slot]
        else:
            lanes = pl.ds(part * LANES, LANES)
            src, dst = num.at[give, lanes], got.at[slot, :, lanes]
        return remote(
            src,
            dst,
            sum_send.at[at],
            sum_recv.at[at],
            (to_chip * 2 + core, to_col),
        )

    for pair in range(pairs):
        attend(pair)
        for i, j in peers:
            sum_copy(i, j, pair).start()
            if pair == pairs - 1:
                sum_copy(i, j, pairs).start()
        if pair == 0:
            until("b", len(jobs) - 1)
    while plan:
        run()

    for i, (dr, dc, cond) in enumerate(halo):

        @pl.when(cond)
        def _():
            halo_copy(i, dr, dc).wait_send()

    z_wait()

    def sent(j):
        for leg in range(4 if j < ff_jobs else 3):
            if leg != 2 or not is_wide(j):
                hop(j, leg).wait_send()
        cond, nxt = onward(j)

        @pl.when(cond)
        def _():
            for across in (False, True) if is_wide(j) else (False,):
                z_pass(j, nxt, across).wait_send()

    for j in range(len(jobs)):
        given(j, functools.partial(sent, j))
    for n in range(pieces):
        tok_copy(n).wait_send()
    tok_out_copy.wait()

    @pl.when(col // 2 == core)
    def _():
        o_copy.wait()

    def own_rows(at_chip, at_col):
        return pl.ds(pl.multiple_of((at_chip * cols + at_col) * share, 16), share)

    def spread(factor):
        parts = []
        for pair in range(pairs):
            lo = jnp.broadcast_to(factor[:, 2 * pair : 2 * pair + 1], (share, LANES))
            hi = jnp.broadcast_to(factor[:, 2 * pair + 1 : 2 * pair + 2], (share, LANES))
            parts.append(jnp.where(lane < HEAD, lo, hi))
        return jnp.concatenate(parts, axis=-1)

    for i, j in peers:
        for part in range(pairs + 1):
            sum_copy(i, j, part).wait_recv()
    mine = own_rows(chip, col)
    slots = [None] + [i * cols + j for i, j in peers]

    def source(slot, lanes):
        value = num[mine, lanes] if slot is None else got[slot, :, lanes]
        return value.astype(jnp.float32)

    stats = []
    for slot in slots:
        s = (stat_out[chip * cols + col] if slot is None else got_stat[slot]).astype(jnp.float32)
        s = jnp.concatenate([s, pltpu.roll(s, HEAD, 1)], axis=0)
        stats.append(s + (pltpu.roll(s, LANES - 16, 1) + pltpu.roll(s, LANES - 32, 1)))
    peak = functools.reduce(jnp.maximum, stats)
    den, total = None, None
    for slot, s in zip(slots, stats):
        factor = jnp.exp(s - peak)
        d = pltpu.roll(s, LANES - 8, 1) * factor
        t = source(slot, pl.ds(0, half)) * spread(factor)
        den = d if den is None else den + d
        total = t if total is None else total + t
    att[core] = total / spread(den)
    n_sum = len(slots) * (pairs + 1)
    swap = remote(att.at[core], att.at[core], sum_send.at[n_sum], sum_recv.at[n_sum], (mate, col))
    swap.start()
    for i, j in peers:
        for part in range(pairs + 1):
            sum_copy(i, j, part).wait_send()
    remote(
        att.at[1 - core], att.at[1 - core], sum_send.at[n_sum], sum_recv.at[n_sum], (mate, col)
    ).wait_recv()
    first, second = att[0], att[1]
    squares = (
        jnp.sum(first * first, axis=-1, keepdims=True)
        + jnp.sum(second * second, axis=-1, keepdims=True)
    ) / depth
    inverse = lax.rsqrt(squares + 1e-06)
    scaled = jnp.concatenate([first, second], axis=-1) * inverse * latent_gain[...][None, :]
    turned = g_o[...].reshape(half, depth)
    done = lax.dot_general(
        scaled.astype(jnp.bfloat16), turned, (((1,), (1,)), ((), ())), preferred_element_type=jnp.float32
    )
    lat[mine, core_lanes] = done.astype(jnp.bfloat16)

    planes = [col] + blocks
    chips = [chip, x_row // 2, y_row // 2, d_row // 2]
    ways = [x_row, y_row, d_row]

    def out_copy_z(k):
        ref = lat.at[mine, core_lanes]
        return remote(ref, ref, out_send.at[k], out_recv.at[col], (row, blocks[k]))

    base_p, base_c = cols, cols + 3 * cols

    def out_copy_plane(n, way):
        ref = lat.at[own_rows(chip, planes[n]), core_lanes]
        at = base_p + n * 3 + way
        return remote(ref, ref, out_send.at[at], out_recv.at[at], (ways[way], col))

    def out_landed_plane(n, way):
        ref = lat.at[own_rows(chips[way + 1], planes[n]), core_lanes]
        at = base_p + n * 3 + way
        return remote(ref, ref, out_send.at[at], out_recv.at[at], (mate, col))

    mate_lanes = pl.ds(pl.multiple_of((1 - core) * half, LANES), half)

    def out_copy_core(n, who, lanes):
        ref = lat.at[own_rows(chips[who], planes[n]), lanes]
        at = base_c + n * 4 + who
        return remote(ref, ref, out_send.at[at], out_recv.at[at], (mate, col))

    def fan(n):
        for way in range(3):
            out_copy_plane(n, way).start()
        out_copy_core(n, 0, core_lanes).start()

    for k in range(cols - 1):
        out_copy_z(k).start()
    fan(0)
    for k in range(cols - 1):
        ref = lat.at[own_rows(chip, blocks[k]), core_lanes]
        remote(ref, ref, out_send.at[0], out_recv.at[blocks[k]], (mate, col)).wait_recv()
        fan(k + 1)
    for n in range(cols):
        for way in range(3):
            out_landed_plane(n, way).wait_recv()
            out_copy_core(n, way + 1, core_lanes).start()
    swap.wait_send()
    for k in range(cols - 1):
        out_copy_z(k).wait_send()
    for n in range(cols):
        for way in range(3):
            out_copy_plane(n, way).wait_send()
    for n in range(cols):
        for who in range(4):
            out_copy_core(n, who, mate_lanes).wait_recv()
            out_copy_core(n, who, core_lanes).wait_send()


def hand_over(tok_in, lat_in, tok, lat, tok_v, lat_v, sem):
    pieces = []
    for src, mid, dst in ((tok_in, tok_v, tok), (lat_in, lat_v, lat)):
        n = src.shape[0] // 2
        for i in range(2):
            at = pl.ds(i * n, n)
            k = 2 * len(pieces)
            pieces.append(
                (
                    pltpu.make_async_copy(src.at[at], mid.at[at], sem.at[k]),
                    pltpu.make_async_copy(mid.at[at], dst.at[at], sem.at[k + 1]),
                )
            )
    for c, _ in pieces:
        c.start()
    for c, d in pieces:
        c.wait()
        d.start()
    for _, d in pieces:
        d.wait()


def hbm(n):
    return [pl.BlockSpec(memory_space=pl.ANY)] * n


def vmem(n):
    return [pl.BlockSpec(memory_space=pltpu.VMEM)] * n


def fits(mesh_rows, mesh_cols, tokens, w_in, w_out, w_kv, queries, w_o):
    height, width, depth = tokens.shape
    return (
        mesh_rows == 8
        and mesh_cols == 4
        and depth == HEADS * HEAD
        and depth % 256 == 0
        and depth % (2 * LANES) == 0
        and w_in.shape[1] % LANES == 0
        and w_out.shape[0] % (32 * mesh_rows) == 0
        and depth % (32 * mesh_rows) == 0
        and w_kv.shape[1] * 2 == depth
        and w_o.shape[1] % 64 == 0
        and w_o.shape[1] * mesh_cols == depth
        and queries.shape[0] % (32 * mesh_rows // 2 * mesh_cols) == 0
        and height % 16 == 0
        and width % 8 == 0
        and height * width % 32 == 0
    )


def kernel_body(tokens, dw_kernel, norm_gain, norm_shift, w_in, w_out, w_kv, queries, latent_gain, w_o):
    rows, cols = lax.axis_size("row"), lax.axis_size("col")
    height, width, depth = tokens.shape
    if not fits(rows, cols, tokens, w_in, w_out, w_kv, queries, w_o):
        return body(
            tokens, dw_kernel, norm_gain, norm_shift, w_in, w_out, w_kv, queries, latent_gain, w_o
        )
    count = height * width
    latents = queries.shape[0]
    f_width = w_in.shape[1]
    half = depth // 2
    bf16, f32 = jnp.bfloat16, jnp.float32

    def cut(w, lead):
        size = w.shape[0]
        for n in lead:
            size //= n
        return w.reshape(lead + (size, w.shape[1]))

    shards = [
        cut(w_in, (2, 2, 2, 2)),
        cut(w_out, (2, 2, 2, 2)),
        cut(w_kv, (2, 2, 2)),
        cut(w_o.T, (2, 2)),
    ]
    share = latents // (rows // 2 * cols)
    pairs = half // LANES
    n_jobs = 4 * (cols - 1) + 4 + 2
    n_sum = rows // 2 * cols * (pairs + 1) + 1
    n_out = cols + 3 * cols + 4 * cols
    dma = pltpu.SemaphoreType.DMA
    outs = pl.pallas_call(
        functools.partial(block_kernel, rows, cols),
        out_shape=(
            jax.ShapeDtypeStruct(tokens.shape, bf16),
            jax.ShapeDtypeStruct((latents, depth), bf16),
        ),
        in_specs=hbm(2) + vmem(2) + hbm(5) + vmem(1),
        out_specs=(hbm(1)[0], vmem(1)[0]),
        scratch_shapes=[
            pltpu.VMEM(tokens.shape, bf16),
            pltpu.VMEM(dw_kernel.shape, f32),
            pltpu.VMEM((latents, half), bf16),
            pltpu.VMEM((cols,) + shards[0].shape, bf16),
            pltpu.VMEM((cols,) + shards[1].shape, bf16),
            pltpu.VMEM((2,) + shards[2].shape, bf16),
            pltpu.VMEM((2,) + shards[3].shape, bf16),
            pltpu.VMEM((height + 2 * HALO, width + 2 * EDGE, depth), f32),
            pltpu.VMEM((height, width, depth), f32),
            pltpu.VMEM((count, depth), bf16),
            pltpu.VMEM((count, f_width), bf16),
            pltpu.VMEM((count, depth), f32),
            pltpu.VMEM((height, width, depth), bf16),
            pltpu.VMEM((2, count, depth), bf16),
            pltpu.VMEM((2, 2 * count, half), bf16),
            pltpu.VMEM((2, HALO, width, depth), bf16),
            pltpu.VMEM((2, HALO, height, depth), bf16),
            pltpu.VMEM((2, HALO, height, depth), bf16),
            pltpu.VMEM((4, HALO, EDGE, depth), bf16),
            pltpu.VMEM((latents, half), bf16),
            pltpu.VMEM((latents, LANES), f32),
            pltpu.VMEM((rows // 2 * cols, share, half), bf16),
            pltpu.VMEM((rows // 2 * cols, share // 2, LANES), bf16),
            pltpu.VMEM((rows // 2 * cols, share // 2, LANES), bf16),
            pltpu.VMEM((2, share, half), f32),
            dma((8,)),
            dma((8,)),
            dma((2 * (14 + n_jobs),)),
            dma((2 * (4 * cols + 6),)),
            dma((n_jobs * 4,)),
            dma((n_jobs * 4,)),
            dma((2,)),
            dma((2,)),
            dma((n_sum,)),
            dma((n_sum,)),
            dma((n_out,)),
            dma((n_out,)),
            dma((8,)),
        ],
        compiler_params=pltpu.CompilerParams(
            collective_id=0, has_side_effects=True, vmem_limit_bytes=VMEM_BYTES
        ),
        name="block",
    )(
        tokens,
        dw_kernel,
        norm_gain,
        norm_shift,
        *shards,
        queries,
        latent_gain,
    )
    return tuple(
        pl.pallas_call(
            hand_over,
            out_shape=tuple(jax.ShapeDtypeStruct(o.shape, o.dtype) for o in outs),
            in_specs=hbm(2),
            out_specs=tuple(hbm(2)),
            scratch_shapes=[pltpu.VMEM(o.shape, o.dtype) for o in outs] + [dma((8,))],
            name="hand_over",
        )(*outs)
    )


def with_halo(cells, sides, width):
    for axis, dim in sides:
        count = lax.axis_size(axis)
        ends = count - 1
        head = lax.slice_in_dim(cells, 0, width, axis=dim)
        tail = lax.slice_in_dim(cells, cells.shape[dim] - width, cells.shape[dim], axis=dim)
        cells = jnp.concatenate(
            [
                lax.ppermute(tail, axis, [(i, (i + 1) % count) for i in range(ends)]),
                cells,
                lax.ppermute(head, axis, [((i + 1) % count, i) for i in range(ends)]),
            ],
            axis=dim,
        )
    return cells


def conv_taps(padded, height, width, dw_kernel):
    mixed = jnp.zeros((height, width, padded.shape[2]), jnp.float32)
    for row_tap in range(7):
        for col_tap in range(7):
            mixed = (
                mixed
                + padded[row_tap : row_tap + height, col_tap : col_tap + width]
                * dw_kernel[row_tap, col_tap]
            )
    return mixed


def layer_norm(mixed, norm_gain, norm_shift):
    center = mixed - jnp.mean(mixed, axis=-1, keepdims=True)
    spread = jnp.mean(center * center, axis=-1, keepdims=True)
    return (center * lax.rsqrt(spread + 1e-06) * norm_gain + norm_shift).astype(jnp.bfloat16)


def finish_latents(numer, denom, latent_gain, w_full):
    attended = (numer / denom[..., None]).reshape(numer.shape[0], -1)
    squares = jnp.mean(attended * attended, axis=-1, keepdims=True)
    scaled = (attended * lax.rsqrt(squares + 1e-06) * latent_gain).astype(jnp.bfloat16)
    return jnp.dot(scaled, w_full, preferred_element_type=jnp.float32).astype(jnp.bfloat16)


def body(tokens, dw_kernel, norm_gain, norm_shift, w_in, w_out, w_kv, queries, latent_gain, w_o):
    height, width, width_d = tokens.shape
    latent_count = queries.shape[0]
    padded = with_halo(tokens, (("row", 0), ("col", 1)), 3)
    mixed = conv_taps(padded.astype(jnp.float32), height, width, dw_kernel)
    normed = layer_norm(mixed, norm_gain, norm_shift).reshape(height * width, width_d)
    residual = tokens.reshape(height * width, width_d).astype(jnp.float32)
    hidden = jax.nn.gelu(
        jnp.dot(
            normed,
            lax.all_gather(w_in, "col", axis=1, tiled=True),
            preferred_element_type=jnp.float32,
        )
    ).astype(jnp.bfloat16)
    update = jnp.dot(
        hidden, lax.all_gather(w_out, "col", axis=0, tiled=True), preferred_element_type=jnp.float32
    )
    token_rows = (residual + update).astype(jnp.bfloat16)
    token_map = token_rows.reshape(height, width, width_d)
    keys_vals = jnp.dot(
        token_rows,
        lax.all_gather(w_kv, "col", axis=1, tiled=True),
        preferred_element_type=jnp.float32,
    ).astype(jnp.bfloat16)
    w_full = lax.all_gather(w_o, "col", axis=1, tiled=True)
    key_heads = keys_vals[:, :width_d].reshape(-1, HEADS, HEAD)
    val_heads = keys_vals[:, width_d:].reshape(-1, HEADS, HEAD)
    query_heads = queries.reshape(latent_count, HEADS, HEAD)
    score_scale = 1.0 / math.sqrt(HEAD)
    group_size = math.gcd(HEADS, 4)
    max_parts, den_parts, num_parts = ([], [], [])
    for first_head in range(0, HEADS, group_size):
        scores = (
            jnp.einsum(
                "lhd,thd->lht",
                query_heads[:, first_head : first_head + group_size],
                key_heads[:, first_head : first_head + group_size],
                preferred_element_type=jnp.float32,
            )
            * score_scale
        )
        local_max = jnp.max(scores, axis=-1)
        weights = jnp.exp(scores - local_max[..., None])
        den_parts.append(jnp.sum(weights, axis=-1))
        max_parts.append(local_max)
        num_parts.append(
            jnp.einsum(
                "lht,thd->lhd",
                weights.astype(jnp.bfloat16),
                val_heads[:, first_head : first_head + group_size],
                preferred_element_type=jnp.float32,
            )
        )
    maxima = jnp.concatenate(max_parts, axis=1)
    denom = jnp.concatenate(den_parts, axis=1)
    numer = jnp.concatenate(num_parts, axis=1)
    peak = lax.pmax(maxima, ("row", "col"))
    factor = jnp.exp(maxima - peak)
    den_terms = denom * factor
    num_terms = (numer * factor[..., None]).reshape(latent_count, width_d)
    den_part, num_part = (
        lax.psum_scatter(den_terms, "col", scatter_dimension=0, tiled=True),
        lax.psum_scatter(num_terms, "col", scatter_dimension=0, tiled=True),
    )
    den_share, num_share = lax.psum((den_part, num_part), "row")
    own_rows = finish_latents(
        num_share.reshape(num_share.shape[0], HEADS, HEAD), den_share, latent_gain, w_full
    )
    latents = lax.all_gather(own_rows, "col", axis=0, tiled=True)
    return (token_map, latents)


def solution(mesh):
    in_specs = (
        P("row", "col", None),
        P(),
        P(),
        P(),
        P(None, "col"),
        P("col", None),
        P(None, "col"),
        P(),
        P(),
        P(None, "col"),
    )
    out_specs = (P("row", "col", None), P())
    return jax.shard_map(kernel_body, mesh=mesh, in_specs=in_specs, out_specs=out_specs, check_vma=False)
```

```python
import functools
import math

import jax
import jax.numpy as jnp
from jax import lax
from jax.experimental import pallas as pl
from jax.experimental.pallas import tpu as pltpu
from jax.sharding import PartitionSpec as P

HEADS = 12
HEAD = 64
HALO = 3
LOG2E = math.log2(math.e)
EDGE = 8
LANES = 128
MESH = pl.DeviceIdType.MESH
VMEM_BYTES = 60 * 1024 * 1024


CONV_PARTS = 4
WIDE = (3, 4, 5)
HALO_AFTER = 4
PRE = 3
Z_LAST = 19
LAG_B = 2
LAG_C = 4


def block_kernel(
    rows,
    cols,
    tokens_in,
    dw_in,
    gain,
    shift,
    w_in,
    w_out,
    w_kv,
    w_o,
    queries_in,
    latent_gain,
    tok_out,
    lat,
    tokens,
    dw,
    queries,
    g_in,
    g_out,
    g_kv,
    g_o,
    pad,
    mixed,
    normed,
    hidden,
    acc,
    tok_map,
    tok_bf,
    kv,
    h_rows,
    h_cols,
    col_out,
    h_corners,
    num,
    stat,
    got,
    stat_out,
    got_stat,
    att,
    halo_send,
    halo_recv,
    z_send,
    z_recv,
    hop_send,
    hop_recv,
    tok_send,
    tok_recv,
    sum_send,
    sum_recv,
    out_send,
    out_recv,
    local_sem,
):
    row, col = lax.axis_index("row"), lax.axis_index("col")
    height, width, depth = tokens.shape
    count = height * width
    y, x, core = row // 4, (row // 2) % 2, row % 2
    chip = row // 2
    half = depth // 2
    x_row = row + 2 * (1 - 2 * x)
    y_row = row + 4 * (1 - 2 * y)
    d_row = row + 2 * (1 - 2 * x) + 4 * (1 - 2 * y)
    mate = row + 1 - 2 * core

    def remote(src, dst, send, recv, device):
        return pltpu.make_async_remote_copy(
            src_ref=src,
            dst_ref=dst,
            send_sem=send,
            recv_sem=recv,
            device_id=device,
            device_id_type=MESH,
        )

    def local(src, dst, i):
        return pltpu.make_async_copy(src, dst, local_sem.at[i])

    core_lanes = pl.ds(pl.multiple_of(core * half, LANES), half)
    tokens_copy = local(tokens_in, tokens, 0)
    dw_copy = local(dw_in, dw, 1)
    queries_copy = local(queries_in.at[:, core_lanes], queries, 2)
    in_copy = local(w_in, g_in.at[col], 3)
    out_copy = local(w_out, g_out.at[col], 4)
    kv_copy = local(w_kv, g_kv.at[col // 2], 5)
    o_copy = local(w_o, g_o.at[col % 2], 6)
    for copy in (tokens_copy, dw_copy, queries_copy, in_copy, out_copy):
        copy.start()

    @pl.when(col % 2 == core)
    def _():
        kv_copy.start()

    @pl.when(col // 2 == core)
    def _():
        o_copy.start()

    both = jnp.minimum(col, cols - 1 - col)
    longer = jnp.where(cols - 1 - col > col, 1, -1)
    blocks = []
    for k in range(cols - 1):
        paired = k < 2 * both
        side = jnp.where(paired, 1 - 2 * (k % 2), longer)
        gap = jnp.where(paired, k // 2 + 1, k - both + 1)
        blocks.append(col + side * gap)

    halo = []
    for dr in (-1, 0, 1):
        for dc in (-1, 0, 1):
            if dr == 0 and dc == 0:
                continue
            cond = None
            for d, pos, n in ((dr, row, rows), (dc, col, cols)):
                if d:
                    one = (pos + d >= 0) & (pos + d < n)
                    cond = one if cond is None else cond & one
            halo.append((dr, dc, cond))

    barrier = pltpu.get_barrier_semaphore()
    peers = [(None, (x_row, col)), (None, (y_row, col)), (None, (mate, col))]
    for dr, dc, cond in halo:
        if dc == 0:
            cond = cond & (row + dr != mate) & (row + dr != x_row) & (row + dr != y_row)
        peers.append((cond, (row + dr, col + dc)))
    greeted = 0
    for cond, device in peers:
        if cond is None:
            pl.semaphore_signal(barrier, inc=1, device_id=device, device_id_type=MESH)
            greeted = greeted + 1
        else:

            @pl.when(cond)
            def _():
                pl.semaphore_signal(barrier, inc=1, device_id=device, device_id_type=MESH)

            greeted = greeted + jnp.where(cond, 1, 0)

    def halo_slot(dr, dc):
        if dc == 0:
            return h_rows.at[0 if dr < 0 else 1]
        if dr == 0:
            return h_cols.at[0 if dc < 0 else 1]
        return h_corners.at[(0 if dr < 0 else 2) + (0 if dc < 0 else 1)]

    def halo_copy(i, dr, dc):
        r_span = {-1: pl.ds(0, HALO), 0: slice(None), 1: pl.ds(height - HALO, HALO)}[dr]
        c_span = {-1: pl.ds(0, EDGE), 0: slice(None), 1: pl.ds(width - EDGE, EDGE)}[dc]
        return remote(
            tokens.at[r_span, c_span] if dr or not dc else col_out.at[0 if dc < 0 else 1],
            halo_slot(-dr, -dc),
            halo_send.at[i],
            halo_recv.at[len(halo) - 1 - i],
            (row + dr, col + dc),
        )

    def own_unit(part, across=False):
        yy, xx = (1 - y, 1 - x) if across else (y, x)
        if part < 4:
            w = (w_in, w_out)[part // 2]
            return w.at[yy, xx, core, part % 2], (g_in, g_out)[part // 2].at[col, yy, xx, core, part % 2]
        if part < 6:
            return w_kv.at[yy, xx, part - 4], g_kv.at[col // 2, yy, xx, part - 4]
        return w_o.at[yy, xx], g_o.at[col % 2, yy, xx]

    def z_id(block, part):
        if part < 4:
            return block * 4 + part
        if part < 6:
            return 4 * cols + (block // 2) * 2 + part - 4
        return 4 * cols + 4 + block % 2

    ff_jobs = 4 * (cols - 1)
    n_send, n_recv = 14 + ff_jobs + 6, 4 * cols + 6

    def z_copies(part, side):
        made = []
        for across in (False, True) if part in WIDE else (False,):
            src, dst = own_unit(part, across)
            at = part * 2 + (0 if side > 0 else 1) + (n_send if across else 0)
            into = z_id(col, part) + (n_recv if across else 0)
            made.append(remote(src, dst, z_send.at[at], z_recv.at[into], (row, col + side)))
        return made

    def z_given(part, side, act):
        cond = (col + side >= 0) & (col + side < cols)
        if part >= 4:
            cond = cond & ((col % 2 if part < 6 else col // 2) == core)

        @pl.when(cond)
        def _():
            for c in z_copies(part, side):
                act(c)

    def z_start(part):
        for side in (-1, 1):
            z_given(part, side, lambda c: c.start())

    def z_wait():
        for part in range(7):
            for side in (-1, 1):
                z_given(part, side, lambda c: c.wait_send())

    near = jnp.where(col < cols // 2, core, core + 2)
    far = jnp.where(col < cols // 2, core + 2, core)
    jobs = [(blocks[k], p) for k in range(cols - 1) for p in range(4)]
    jobs += [(near, 4), (near, 5), (far, 4), (far, 5)]
    jobs += [(core * 2, 6), (core * 2 + 1, 6)]

    def unit(j, dy, dx):
        block, part = jobs[j]
        yy, xx = (1 - y if dy else y), (1 - x if dx else x)
        if part < 4:
            return (g_in, g_out)[part // 2].at[block, yy, xx, core, part % 2]
        if part < 6:
            return g_kv.at[block // 2, yy, xx, part - 4]
        return g_o.at[block % 2, yy, xx]

    def turn(j):
        part = jobs[j][1]
        return j % 2 if part == 6 or 3 in WIDE else part % 2

    def hop(j, leg):
        at = j * 4 + leg
        if leg == 3:
            block, part = jobs[j]
            ref = (g_in, g_out)[part // 2].at[block, :, :, core, part % 2]
            device = mate
        elif leg == 2:
            ref = unit(j, 0, 1) if turn(j) == 0 else unit(j, 1, 0)
            device = y_row if turn(j) == 0 else x_row
        else:
            ref = unit(j, 0, 0)
            device = x_row if leg == 0 else y_row
        return remote(ref, ref, hop_send.at[at], hop_recv.at[at], (device, col))

    def landed(j, leg):
        at = j * 4 + leg
        if leg == 3:
            block, part = jobs[j]
            ref = (g_in, g_out)[part // 2].at[block, :, :, 1 - core, part % 2]
        elif leg == 2:
            ref = unit(j, 1, 1)
        else:
            ref = unit(j, 0, 1) if leg == 0 else unit(j, 1, 0)
        return remote(ref, ref, hop_send.at[at], hop_recv.at[at], (mate, col))

    def onward(j):
        block = jobs[j][0]
        nxt = col + jnp.where(col > block, 1, -1)
        return (block != col) & (nxt >= 0) & (nxt < cols), nxt

    def is_wide(j):
        return jobs[j][1] in WIDE

    def z_arrival(j, across=False):
        block, part = jobs[j]
        ref = unit(j, 1, 1) if across else unit(j, 0, 0)
        at = z_id(block, part) + (n_recv if across else 0)
        return remote(ref, ref, z_send.at[0], z_recv.at[at], (mate, col))

    def z_pass(j, nxt, across=False):
        block, part = jobs[j]
        ref = unit(j, 1, 1) if across else unit(j, 0, 0)
        at = z_id(block, part) + (n_recv if across else 0)
        by = 14 + j + (n_send if across else 0)
        return remote(ref, ref, z_send.at[by], z_recv.at[at], (row, nxt))

    def step_z(j, gap=None):
        cond, nxt = onward(j)
        if gap is not None:
            block = jobs[j][0]
            cond = cond & (jnp.where(col > block, col - block, block - col) == gap)

        @pl.when(cond)
        def _():
            for across in (False, True) if is_wide(j) else (False,):
                z_arrival(j, across).wait_recv()
                z_pass(j, nxt, across).start()

    def given(j, act):
        if j < ff_jobs:
            act()
        else:
            pl.when(jobs[j][0] != col)(act)

    def step_a(j):
        @pl.when(jnp.logical_not(onward(j)[0]))
        def _():
            z_arrival(j).wait_recv()

        hop(j, 0).start()
        hop(j, 1).start()

    def step_b(j):
        if not is_wide(j):
            landed(j, turn(j)).wait_recv()
            hop(j, 2).start()

    def step_c(j):
        if is_wide(j):
            landed(j, 0).wait_recv()
            landed(j, 1).wait_recv()

            @pl.when(jnp.logical_not(onward(j)[0]))
            def _():
                z_arrival(j, True).wait_recv()

        else:
            landed(j, 1 - turn(j)).wait_recv()
            landed(j, 2).wait_recv()
        if j < ff_jobs:
            hop(j, 3).start()

    last = ff_jobs + 4
    z_starts = {p: p - 2 for p in range(max(HALO_AFTER, 2), 4)} | {4: 4, 5: 5, 6: 9}
    passes = [(4 * r + p, p + (0, 1, 3)[r], None) for r in range(cols - 1) for p in range(4)]
    passes += [(ff_jobs, 8, None), (ff_jobs + 1, 9, None), (ff_jobs + 2, 10, None), (ff_jobs + 3, 11, None)]
    passes += [(last + i, 14 + 3 * d, d + 1) for i in range(2) for d in range(2)]

    def z_tick(t):
        for part, at in z_starts.items():
            if at == t:
                z_start(part)
        for j, at, gap in passes:
            if at == t:
                step_z(j, gap)

    steps = {"z": z_tick, "a": step_a, "b": step_b, "c": step_c}
    plan = []
    for t in range(last):
        plan.append(("z", t))
        for name, lag in (("a", 0), ("b", LAG_B), ("c", LAG_C)):
            if t - lag >= 0:
                plan.append((name, t - lag))
        plan.append(("tick", t))
    for t in range(last, last + LAG_B):
        plan.append(("z", t))
        plan.append(("b", t - LAG_B))
        if t - LAG_C >= 0:
            plan.append(("c", t - LAG_C))
    for t in range(last + LAG_B, Z_LAST):
        plan.append(("z", t))
    plan += [("a", j) for j in range(last, len(jobs))]
    plan += [("c", j) for j in range(last + LAG_B - LAG_C, last)]
    plan += [("b", j) for j in range(last, len(jobs))]
    plan += [("c", j) for j in range(last, len(jobs))]

    def run():
        name, j = plan.pop(0)
        if name == "z":
            z_tick(j)
        elif name != "tick":
            given(j, functools.partial(steps[name], j))
        return name, j

    def tick():
        while plan and run()[0] != "tick":
            pass

    def until(name, j):
        while (name, j) in plan:
            run()

    def finish(j):
        until("c", j)
        if j < ff_jobs:
            landed(j, 3).wait_recv()

    tokens_copy.wait()
    pad[pl.ds(HALO, height), pl.ds(EDGE, width), :] = tokens[...].astype(jnp.float32)
    for side in range(2):
        edge = pl.ds(side * (EDGE + width), EDGE)
        pad[pl.ds(HALO, height), edge, :] = jnp.zeros((height, EDGE, depth), jnp.float32)
        for n in range(HALO):
            at = EDGE + (n if side == 0 else width - HALO + n)
            col_out[side, n] = pad[pl.ds(HALO, height), at, :].astype(jnp.bfloat16)
    pl.semaphore_wait(barrier, greeted)

    for part in range(HALO_AFTER):
        z_start(part)
    for i, (dr, dc, cond) in enumerate(halo):

        @pl.when(cond)
        def _():
            halo_copy(i, dr, dc).start()

    for part in range(HALO_AFTER, 2):
        z_start(part)
    for _ in range(PRE):
        tick()

    spans = {-1: (0, HALO), 0: (HALO, height), 1: (HALO + height, HALO)}
    lanes_of = {-1: (0, EDGE), 0: (EDGE, width), 1: (EDGE + width, EDGE)}
    for i, (dr, dc, cond) in enumerate(halo):
        r0, rn = spans[dr]
        c0, cn = lanes_of[dc]

        @pl.when(cond)
        def _():
            halo_copy(len(halo) - 1 - i, -dr, -dc).wait_recv()
            if dr == 0:
                for n in range(HALO):
                    at = EDGE - HALO + n if dc < 0 else EDGE + width + n
                    side = 0 if dc < 0 else 1
                    pad[pl.ds(HALO, height), at, :] = h_cols[side, n].astype(jnp.float32)
            else:
                pad[pl.ds(r0, rn), pl.ds(c0, cn), :] = halo_slot(dr, dc)[...].astype(jnp.float32)

        if dr:

            @pl.when(jnp.logical_not(cond))
            def _():
                pad[pl.ds(r0, rn), pl.ds(c0, cn), :] = jnp.zeros((rn, cn, depth), jnp.float32)

    taps = 2 * HALO + 1
    chunks = depth // LANES
    dw_copy.wait()

    def conv_rows(first, n_rows):
        def one(step, carry):
            i = first + step // chunks
            q = pl.multiple_of((step % chunks) * LANES, LANES)
            sums = [None] * taps
            for a in range(taps):
                line = pad[i + a, :, pl.ds(q, LANES)]
                for b in range(taps):
                    lo = 0 if b < HALO else EDGE
                    hi = EDGE + width + (EDGE if b > HALO else 0)
                    term = line[lo:hi] * dw[a, pl.ds(b, 1), pl.ds(q, LANES)]
                    sums[b] = term if sums[b] is None else sums[b] + term
            total = sums[HALO]
            for b in range(taps):
                if b == HALO:
                    continue
                size = width + EDGE
                offset = EDGE - HALO + b - (0 if b < HALO else EDGE)
                total = total + pltpu.roll(sums[b], (size - offset) % size, 0)[:width]
            mixed[i, :, pl.ds(q, LANES)] = total
            return carry

        lax.fori_loop(0, n_rows * chunks, one, 0, unroll=2)

    group = 2
    span = group * width

    def norm_rows(g, carry):
        value = mixed[pl.ds(g * group, group), :, :].reshape(span, depth)
        center = value - jnp.mean(value, axis=-1, keepdims=True)
        spread = jnp.mean(center * center, axis=-1, keepdims=True)
        out = center * lax.rsqrt(spread + 1e-06) * gain[...][None, :] + shift[...][None, :]
        normed[pl.ds(pl.multiple_of(g * span, 16), span), :] = out.astype(jnp.bfloat16)
        return carry

    tick()
    parts = CONV_PARTS
    for part in range(parts):
        conv_rows(part * (height // parts), height // parts)
        tick()
    half_groups = height // group // 2
    lax.fori_loop(0, half_groups, norm_rows, 0)
    tick()
    lax.fori_loop(half_groups, 2 * half_groups, norm_rows, 0)
    tick()
    in_copy.wait()
    out_copy.wait()

    def wide(ref, block, lo, size):
        value = ref[(block,) + (slice(None),) * (len(ref.shape) - 2) + (pl.ds(lo, size),)]
        return value.reshape(-1, size)

    f_width = w_in.shape[-1]
    tile = 256 if f_width % 256 == 0 else LANES

    def expand(block):
        def one(n, carry):
            lo = pl.multiple_of(n * tile, tile)
            u = jnp.dot(normed[...], wide(g_in, block, lo, tile), preferred_element_type=jnp.float32)
            hidden[:, pl.ds(lo, tile)] = jax.nn.gelu(u).astype(jnp.bfloat16)
            return carry

        lax.fori_loop(0, f_width // tile, one, 0, unroll=True)

    def contract(block, fresh):
        def one(n, carry):
            lo = pl.multiple_of(n * 256, 256)
            part = jnp.dot(
                hidden[...], wide(g_out, block, lo, 256), preferred_element_type=jnp.float32
            )
            if fresh:
                acc[:, pl.ds(lo, 256)] = part
            else:
                acc[:, pl.ds(lo, 256)] += part
            return carry

        lax.fori_loop(0, depth // 256, one, 0, unroll=True)

    expand(col)
    tick()
    contract(col, True)
    tick()
    for k in range(cols - 1):
        finish(4 * k)
        finish(4 * k + 1)
        expand(blocks[k])
        finish(4 * k + 2)
        finish(4 * k + 3)
        contract(blocks[k], False)

    def close_rows(g, carry):
        base = pad[pl.ds(HALO + g * group, group), pl.ds(EDGE, width), :].reshape(span, depth)
        at = pl.ds(pl.multiple_of(g * span, 16), span)
        total = base + acc[at, :]
        tok_map[pl.ds(g * group, group), :, :] = total.reshape(group, width, depth).astype(jnp.bfloat16)
        tok_bf[0, at, :] = total.astype(jnp.bfloat16)
        return carry

    pieces = 2
    piece = count // pieces

    def tok_copy(n):
        at = pl.ds(n * piece, piece)
        return remote(tok_bf.at[0, at], tok_bf.at[1, at], tok_send.at[n], tok_recv.at[n], (mate, col))

    for n in range(pieces):
        lax.fori_loop(n * (height // group // pieces), (n + 1) * (height // group // pieces), close_rows, 0)
        tok_copy(n).start()
    tok_out_copy = local(tok_map, tok_out, 7)
    tok_out_copy.start()

    kv_width = w_kv.shape[-1]

    def project(block, side):
        out = jnp.dot(
            tok_bf[side], wide(g_kv, block // 2, 0, kv_width), preferred_element_type=jnp.float32
        )
        kv[block // 2, pl.ds(side * count, count), :] = out.astype(jnp.bfloat16)

    @pl.when(col % 2 == core)
    def _():
        kv_copy.wait()

    finish(ff_jobs)
    finish(ff_jobs + 1)
    project(near, 0)
    for n in range(pieces):
        tok_copy(n).wait_recv()
    project(near, 1)
    finish(ff_jobs + 2)
    finish(ff_jobs + 3)
    for side in range(2):
        project(far, side)
    queries_copy.wait()

    latents = queries.shape[0]
    scale = 1.0 / math.sqrt(HEAD)
    lane = lax.broadcasted_iota(jnp.int32, (1, LANES), 1)
    pairs = half // LANES
    step_rows = latents
    share = latents // (rows // 2 * cols)

    def attend(pair):
        lanes = pl.ds(pair * LANES, LANES)

        def one(n, carry):
            at = pl.ds(pl.multiple_of(n * step_rows, 16), step_rows)
            q = queries[at, lanes]
            keys = kv[0, :, lanes]
            vals = kv[1, :, lanes]
            base = jnp.zeros((step_rows, LANES), jnp.float32) if pair == 0 else stat[at, :]
            outs = []
            for s in range(2):
                keep = (lane // HEAD) == s
                q_one = jnp.where(keep, q, jnp.zeros_like(q))
                scores = lax.dot_general(
                    q_one, keys, (((1,), (1,)), ((), ())), preferred_element_type=jnp.float32
                )
                top = jnp.max(scores, axis=-1, keepdims=True)
                weights = jnp.exp2((scores - top) * (scale * LOG2E))
                vals_one = jnp.where(keep, vals, jnp.ones_like(vals))
                out = jnp.dot(
                    weights.astype(jnp.bfloat16), vals_one, preferred_element_type=jnp.float32
                )
                outs.append(out)
                base = jnp.where(lane == pair * 2 + s, top * scale, base)
                base = jnp.where(lane == pair * 2 + s + 8 + HEAD * (1 - s), out, base)
            num[at, lanes] = jnp.where(lane < HEAD, outs[0], outs[1]).astype(jnp.bfloat16)
            if pair < pairs - 1:
                stat[at, :] = base
            else:
                base = jnp.where(lane < 16, base + pltpu.roll(base, HEAD, 1), 0.0)
                high = base.astype(jnp.bfloat16).astype(jnp.float32)
                rest = base - high
                mid = rest.astype(jnp.bfloat16).astype(jnp.float32)
                low = rest - mid
                out = high + pltpu.roll(mid, 16, 1) + pltpu.roll(low, 32, 1)
                out = out.reshape(-1, share, LANES)
                packed = out[:, : share // 2] + pltpu.roll(out[:, share // 2 :], HEAD, 2)
                owners = step_rows // share
                stat_out[pl.ds(n * owners, owners)] = packed.astype(jnp.bfloat16)
            return carry

        lax.fori_loop(0, latents // step_rows, one, 0)

    peers = [(i, j) for j in (*range(1, cols), 0) for i in range(rows // 2) if i or j]

    def sum_copy(i, j, part):
        to_chip, to_col = (chip + i) % (rows // 2), (col + j) % cols
        slot = i * cols + j
        give = pl.ds(pl.multiple_of((to_chip * cols + to_col) * share, 16), share)
        at = slot * (pairs + 1) + part
        if part == pairs:
            src, dst = stat_out.at[to_chip * cols + to_col], got_stat.at[slot]
        else:
            lanes = pl.ds(part * LANES, LANES)
            src, dst = num.at[give, lanes], got.at[slot, :, lanes]
        return remote(
            src,
            dst,
            sum_send.at[at],
            sum_recv.at[at],
            (to_chip * 2 + core, to_col),
        )

    for pair in range(pairs):
        attend(pair)
        for i, j in peers:
            sum_copy(i, j, pair).start()
            if pair == pairs - 1:
                sum_copy(i, j, pairs).start()
        if pair == 0:
            until("b", len(jobs) - 1)
    while plan:
        run()

    for i, (dr, dc, cond) in enumerate(halo):

        @pl.when(cond)
        def _():
            halo_copy(i, dr, dc).wait_send()

    z_wait()

    def sent(j):
        for leg in range(4 if j < ff_jobs else 3):
            if leg != 2 or not is_wide(j):
                hop(j, leg).wait_send()
        cond, nxt = onward(j)

        @pl.when(cond)
        def _():
            for across in (False, True) if is_wide(j) else (False,):
                z_pass(j, nxt, across).wait_send()

    for j in range(len(jobs)):
        given(j, functools.partial(sent, j))
    for n in range(pieces):
        tok_copy(n).wait_send()
    tok_out_copy.wait()

    @pl.when(col // 2 == core)
    def _():
        o_copy.wait()

    def own_rows(at_chip, at_col):
        return pl.ds(pl.multiple_of((at_chip * cols + at_col) * share, 16), share)

    def spread(factor):
        parts = []
        for pair in range(pairs):
            lo = jnp.broadcast_to(factor[:, 2 * pair : 2 * pair + 1], (share, LANES))
            hi = jnp.broadcast_to(factor[:, 2 * pair + 1 : 2 * pair + 2], (share, LANES))
            parts.append(jnp.where(lane < HEAD, lo, hi))
        return jnp.concatenate(parts, axis=-1)

    for i, j in peers:
        for part in range(pairs + 1):
            sum_copy(i, j, part).wait_recv()
    mine = own_rows(chip, col)
    slots = [None] + [i * cols + j for i, j in peers]

    def source(slot, lanes):
        value = num[mine, lanes] if slot is None else got[slot, :, lanes]
        return value.astype(jnp.float32)

    stats = []
    for slot in slots:
        s = (stat_out[chip * cols + col] if slot is None else got_stat[slot]).astype(jnp.float32)
        s = jnp.concatenate([s, pltpu.roll(s, HEAD, 1)], axis=0)
        stats.append(s + (pltpu.roll(s, LANES - 16, 1) + pltpu.roll(s, LANES - 32, 1)))
    peak = functools.reduce(jnp.maximum, stats)
    den, total = None, None
    for slot, s in zip(slots, stats):
        factor = jnp.exp(s - peak)
        d = pltpu.roll(s, LANES - 8, 1) * factor
        t = source(slot, pl.ds(0, half)) * spread(factor)
        den = d if den is None else den + d
        total = t if total is None else total + t
    att[core] = total / spread(den)
    n_sum = len(slots) * (pairs + 1)
    swap = remote(att.at[core], att.at[core], sum_send.at[n_sum], sum_recv.at[n_sum], (mate, col))
    swap.start()
    for i, j in peers:
        for part in range(pairs + 1):
            sum_copy(i, j, part).wait_send()
    remote(
        att.at[1 - core], att.at[1 - core], sum_send.at[n_sum], sum_recv.at[n_sum], (mate, col)
    ).wait_recv()
    first, second = att[0], att[1]
    squares = (
        jnp.sum(first * first, axis=-1, keepdims=True)
        + jnp.sum(second * second, axis=-1, keepdims=True)
    ) / depth
    inverse = lax.rsqrt(squares + 1e-06)
    scaled = jnp.concatenate([first, second], axis=-1) * inverse * latent_gain[...][None, :]
    turned = g_o[...].reshape(half, depth)
    done = lax.dot_general(
        scaled.astype(jnp.bfloat16), turned, (((1,), (1,)), ((), ())), preferred_element_type=jnp.float32
    )
    lat[mine, core_lanes] = done.astype(jnp.bfloat16)

    planes = [col] + blocks
    chips = [chip, x_row // 2, y_row // 2, d_row // 2]
    ways = [x_row, y_row, d_row]

    def out_copy_z(k):
        ref = lat.at[mine, core_lanes]
        return remote(ref, ref, out_send.at[k], out_recv.at[col], (row, blocks[k]))

    base_p, base_c = cols, cols + 3 * cols

    def out_copy_plane(n, way):
        ref = lat.at[own_rows(chip, planes[n]), core_lanes]
        at = base_p + n * 3 + way
        return remote(ref, ref, out_send.at[at], out_recv.at[at], (ways[way], col))

    def out_landed_plane(n, way):
        ref = lat.at[own_rows(chips[way + 1], planes[n]), core_lanes]
        at = base_p + n * 3 + way
        return remote(ref, ref, out_send.at[at], out_recv.at[at], (mate, col))

    mate_lanes = pl.ds(pl.multiple_of((1 - core) * half, LANES), half)

    def out_copy_core(n, who, lanes):
        ref = lat.at[own_rows(chips[who], planes[n]), lanes]
        at = base_c + n * 4 + who
        return remote(ref, ref, out_send.at[at], out_recv.at[at], (mate, col))

    def fan(n):
        for way in range(3):
            out_copy_plane(n, way).start()
        out_copy_core(n, 0, core_lanes).start()

    for k in range(cols - 1):
        out_copy_z(k).start()
    fan(0)
    for k in range(cols - 1):
        ref = lat.at[own_rows(chip, blocks[k]), core_lanes]
        remote(ref, ref, out_send.at[0], out_recv.at[blocks[k]], (mate, col)).wait_recv()
        fan(k + 1)
    for n in range(cols):
        for way in range(3):
            out_landed_plane(n, way).wait_recv()
            out_copy_core(n, way + 1, core_lanes).start()
    swap.wait_send()
    for k in range(cols - 1):
        out_copy_z(k).wait_send()
    for n in range(cols):
        for way in range(3):
            out_copy_plane(n, way).wait_send()
    for n in range(cols):
        for who in range(4):
            out_copy_core(n, who, mate_lanes).wait_recv()
            out_copy_core(n, who, core_lanes).wait_send()


def hand_over(tok_in, lat_in, tok, lat, tok_v, lat_v, sem):
    pieces = []
    for src, mid, dst in ((tok_in, tok_v, tok), (lat_in, lat_v, lat)):
        n = src.shape[0] // 2
        for i in range(2):
            at = pl.ds(i * n, n)
            k = 2 * len(pieces)
            pieces.append(
                (
                    pltpu.make_async_copy(src.at[at], mid.at[at], sem.at[k]),
                    pltpu.make_async_copy(mid.at[at], dst.at[at], sem.at[k + 1]),
                )
            )
    for c, _ in pieces:
        c.start()
    for c, d in pieces:
        c.wait()
        d.start()
    for _, d in pieces:
        d.wait()


def hbm(n):
    return [pl.BlockSpec(memory_space=pl.ANY)] * n


def vmem(n):
    return [pl.BlockSpec(memory_space=pltpu.VMEM)] * n


def fits(mesh_rows, mesh_cols, tokens, w_in, w_out, w_kv, queries, w_o):
    height, width, depth = tokens.shape
    return (
        mesh_rows == 8
        and mesh_cols == 4
        and depth == HEADS * HEAD
        and depth % 256 == 0
        and depth % (2 * LANES) == 0
        and w_in.shape[1] % LANES == 0
        and w_out.shape[0] % (32 * mesh_rows) == 0
        and depth % (32 * mesh_rows) == 0
        and w_kv.shape[1] * 2 == depth
        and w_o.shape[1] % 64 == 0
        and w_o.shape[1] * mesh_cols == depth
        and queries.shape[0] % (32 * mesh_rows // 2 * mesh_cols) == 0
        and height % 16 == 0
        and width % 8 == 0
        and height * width % 32 == 0
    )


def kernel_body(tokens, dw_kernel, norm_gain, norm_shift, w_in, w_out, w_kv, queries, latent_gain, w_o):
    rows, cols = lax.axis_size("row"), lax.axis_size("col")
    height, width, depth = tokens.shape
    if not fits(rows, cols, tokens, w_in, w_out, w_kv, queries, w_o):
        return body(
            tokens, dw_kernel, norm_gain, norm_shift, w_in, w_out, w_kv, queries, latent_gain, w_o
        )
    count = height * width
    latents = queries.shape[0]
    f_width = w_in.shape[1]
    half = depth // 2
    bf16, f32 = jnp.bfloat16, jnp.float32

    def cut(w, lead):
        size = w.shape[0]
        for n in lead:
            size //= n
        return w.reshape(lead + (size, w.shape[1]))

    shards = [
        cut(w_in, (2, 2, 2, 2)),
        cut(w_out, (2, 2, 2, 2)),
        cut(w_kv, (2, 2, 2)),
        cut(w_o.T, (2, 2)),
    ]
    share = latents // (rows // 2 * cols)
    pairs = half // LANES
    n_jobs = 4 * (cols - 1) + 4 + 2
    n_sum = rows // 2 * cols * (pairs + 1) + 1
    n_out = cols + 3 * cols + 4 * cols
    dma = pltpu.SemaphoreType.DMA
    outs = pl.pallas_call(
        functools.partial(block_kernel, rows, cols),
        out_shape=(
            jax.ShapeDtypeStruct(tokens.shape, bf16),
            jax.ShapeDtypeStruct((latents, depth), bf16),
        ),
        in_specs=hbm(2) + vmem(2) + hbm(5) + vmem(1),
        out_specs=(hbm(1)[0], vmem(1)[0]),
        scratch_shapes=[
            pltpu.VMEM(tokens.shape, bf16),
            pltpu.VMEM(dw_kernel.shape, f32),
            pltpu.VMEM((latents, half), bf16),
            pltpu.VMEM((cols,) + shards[0].shape, bf16),
            pltpu.VMEM((cols,) + shards[1].shape, bf16),
            pltpu.VMEM((2,) + shards[2].shape, bf16),
            pltpu.VMEM((2,) + shards[3].shape, bf16),
            pltpu.VMEM((height + 2 * HALO, width + 2 * EDGE, depth), f32),
            pltpu.VMEM((height, width, depth), f32),
            pltpu.VMEM((count, depth), bf16),
            pltpu.VMEM((count, f_width), bf16),
            pltpu.VMEM((count, depth), f32),
            pltpu.VMEM((height, width, depth), bf16),
            pltpu.VMEM((2, count, depth), bf16),
            pltpu.VMEM((2, 2 * count, half), bf16),
            pltpu.VMEM((2, HALO, width, depth), bf16),
            pltpu.VMEM((2, HALO, height, depth), bf16),
            pltpu.VMEM((2, HALO, height, depth), bf16),
            pltpu.VMEM((4, HALO, EDGE, depth), bf16),
            pltpu.VMEM((latents, half), bf16),
            pltpu.VMEM((latents, LANES), f32),
            pltpu.VMEM((rows // 2 * cols, share, half), bf16),
            pltpu.VMEM((rows // 2 * cols, share // 2, LANES), bf16),
            pltpu.VMEM((rows // 2 * cols, share // 2, LANES), bf16),
            pltpu.VMEM((2, share, half), f32),
            dma((8,)),
            dma((8,)),
            dma((2 * (14 + n_jobs),)),
            dma((2 * (4 * cols + 6),)),
            dma((n_jobs * 4,)),
            dma((n_jobs * 4,)),
            dma((2,)),
            dma((2,)),
            dma((n_sum,)),
            dma((n_sum,)),
            dma((n_out,)),
            dma((n_out,)),
            dma((8,)),
        ],
        compiler_params=pltpu.CompilerParams(
            collective_id=0, has_side_effects=True, vmem_limit_bytes=VMEM_BYTES
        ),
        name="block",
    )(
        tokens,
        dw_kernel,
        norm_gain,
        norm_shift,
        *shards,
        queries,
        latent_gain,
    )
    return tuple(
        pl.pallas_call(
            hand_over,
            out_shape=tuple(jax.ShapeDtypeStruct(o.shape, o.dtype) for o in outs),
            in_specs=hbm(2),
            out_specs=tuple(hbm(2)),
            scratch_shapes=[pltpu.VMEM(o.shape, o.dtype) for o in outs] + [dma((8,))],
            name="hand_over",
        )(*outs)
    )


def with_halo(cells, sides, width):
    for axis, dim in sides:
        count = lax.axis_size(axis)
        ends = count - 1
        head = lax.slice_in_dim(cells, 0, width, axis=dim)
        tail = lax.slice_in_dim(cells, cells.shape[dim] - width, cells.shape[dim], axis=dim)
        cells = jnp.concatenate(
            [
                lax.ppermute(tail, axis, [(i, (i + 1) % count) for i in range(ends)]),
                cells,
                lax.ppermute(head, axis, [((i + 1) % count, i) for i in range(ends)]),
            ],
            axis=dim,
        )
    return cells


def conv_taps(padded, height, width, dw_kernel):
    mixed = jnp.zeros((height, width, padded.shape[2]), jnp.float32)
    for row_tap in range(7):
        for col_tap in range(7):
            mixed = (
                mixed
                + padded[row_tap : row_tap + height, col_tap : col_tap + width]
                * dw_kernel[row_tap, col_tap]
            )
    return mixed


def layer_norm(mixed, norm_gain, norm_shift):
    center = mixed - jnp.mean(mixed, axis=-1, keepdims=True)
    spread = jnp.mean(center * center, axis=-1, keepdims=True)
    return (center * lax.rsqrt(spread + 1e-06) * norm_gain + norm_shift).astype(jnp.bfloat16)


def finish_latents(numer, denom, latent_gain, w_full):
    attended = (numer / denom[..., None]).reshape(numer.shape[0], -1)
    squares = jnp.mean(attended * attended, axis=-1, keepdims=True)
    scaled = (attended * lax.rsqrt(squares + 1e-06) * latent_gain).astype(jnp.bfloat16)
    return jnp.dot(scaled, w_full, preferred_element_type=jnp.float32).astype(jnp.bfloat16)


def body(tokens, dw_kernel, norm_gain, norm_shift, w_in, w_out, w_kv, queries, latent_gain, w_o):
    height, width, width_d = tokens.shape
    latent_count = queries.shape[0]
    padded = with_halo(tokens, (("row", 0), ("col", 1)), 3)
    mixed = conv_taps(padded.astype(jnp.float32), height, width, dw_kernel)
    normed = layer_norm(mixed, norm_gain, norm_shift).reshape(height * width, width_d)
    residual = tokens.reshape(height * width, width_d).astype(jnp.float32)
    hidden = jax.nn.gelu(
        jnp.dot(
            normed,
            lax.all_gather(w_in, "col", axis=1, tiled=True),
            preferred_element_type=jnp.float32,
        )
    ).astype(jnp.bfloat16)
    update = jnp.dot(
        hidden, lax.all_gather(w_out, "col", axis=0, tiled=True), preferred_element_type=jnp.float32
    )
    token_rows = (residual + update).astype(jnp.bfloat16)
    token_map = token_rows.reshape(height, width, width_d)
    keys_vals = jnp.dot(
        token_rows,
        lax.all_gather(w_kv, "col", axis=1, tiled=True),
        preferred_element_type=jnp.float32,
    ).astype(jnp.bfloat16)
    w_full = lax.all_gather(w_o, "col", axis=1, tiled=True)
    key_heads = keys_vals[:, :width_d].reshape(-1, HEADS, HEAD)
    val_heads = keys_vals[:, width_d:].reshape(-1, HEADS, HEAD)
    query_heads = queries.reshape(latent_count, HEADS, HEAD)
    score_scale = 1.0 / math.sqrt(HEAD)
    group_size = math.gcd(HEADS, 4)
    max_parts, den_parts, num_parts = ([], [], [])
    for first_head in range(0, HEADS, group_size):
        scores = (
            jnp.einsum(
                "lhd,thd->lht",
                query_heads[:, first_head : first_head + group_size],
                key_heads[:, first_head : first_head + group_size],
                preferred_element_type=jnp.float32,
            )
            * score_scale
        )
        local_max = jnp.max(scores, axis=-1)
        weights = jnp.exp(scores - local_max[..., None])
        den_parts.append(jnp.sum(weights, axis=-1))
        max_parts.append(local_max)
        num_parts.append(
            jnp.einsum(
                "lht,thd->lhd",
                weights.astype(jnp.bfloat16),
                val_heads[:, first_head : first_head + group_size],
                preferred_element_type=jnp.float32,
            )
        )
    maxima = jnp.concatenate(max_parts, axis=1)
    denom = jnp.concatenate(den_parts, axis=1)
    numer = jnp.concatenate(num_parts, axis=1)
    peak = lax.pmax(maxima, ("row", "col"))
    factor = jnp.exp(maxima - peak)
    den_terms = denom * factor
    num_terms = (numer * factor[..., None]).reshape(latent_count, width_d)
    den_part, num_part = (
        lax.psum_scatter(den_terms, "col", scatter_dimension=0, tiled=True),
        lax.psum_scatter(num_terms, "col", scatter_dimension=0, tiled=True),
    )
    den_share, num_share = lax.psum((den_part, num_part), "row")
    own_rows = finish_latents(
        num_share.reshape(num_share.shape[0], HEADS, HEAD), den_share, latent_gain, w_full
    )
    latents = lax.all_gather(own_rows, "col", axis=0, tiled=True)
    return (token_map, latents)


def solution(mesh):
    in_specs = (
        P("row", "col", None),
        P(),
        P(),
        P(),
        P(None, "col"),
        P("col", None),
        P(None, "col"),
        P(),
        P(),
        P(None, "col"),
    )
    out_specs = (P("row", "col", None), P())
    return jax.shard_map(kernel_body, mesh=mesh, in_specs=in_specs, out_specs=out_specs, check_vma=False)
```
